128 devices in a mesh: gx: 8 (over z, core), gy: 16 (over y, x).
Axes of the slice: x: 4, y: 4, z: 4, core: 2. Of those that a mesh axis runs over, the one named last changes fastest.
Arguments:
- queries: bfloat16 [2048, 1536], P(('gx', 'gy')), may hold values from -40 to 40
- new_kv: bfloat16 [2048, 1024], P(('gx', 'gy')), may hold values from -6 to 6
- cache_pool: bfloat16 [16384, 16, 1024], P(('gx', 'gy')), may hold values from -6 to 6
- cache_len: int32 [2048], P(('gx', 'gy')), may hold values from 1 to 512, as said below
- local_pages: int32 [1024, 32], P(('gx', 'gy')), may hold values from 0 to 127
- anchor: int32 [1024], P(('gx', 'gy')), may hold values from 0 to 15, as said below
- push_pages: int32 [2048, 32], P(('gx', 'gy')), may hold values from 0 to 127
- prefill_attn: bfloat16 [14336, 1536], P(('gx', 'gy')), may hold values from -4 to 4
- residual: bfloat16 [16384, 1536], P(('gx', 'gy')), may hold values from -7 to 7
- out_weight: bfloat16 [1536, 1536], P('gx'), may hold values from -0.15625 to 0.15625
- norm_gain: bfloat16 [1536], replicated, may hold values from 0.099609375 to 1.8984375
- router: bfloat16 [1536, 32], replicated, may hold values from -4 to 4
- routes: int32 [16384, 8], P(('gx', 'gy')), may hold values from 0 to 31, all different within a row; in each aligned block of 128 rows (0 to 127, 128 to 255, ...) at most 48 rows name the same one
- gate_up: bfloat16 [1536, 32, 1024], P('gx', 'gy'), may hold values from -0.15625 to 0.15625
- down_proj: bfloat16 [1536, 32, 512], P('gx', 'gy'), may hold values from -0.25 to 0.25
Outputs:
- attended: bfloat16 [2048, 1536], P(('gx', 'gy'))
- layer_out: float32 [16384, 1536], P(('gx', 'gy'))
The draws below stay inside these ranges and needn't reach their ends.
Inputs may be any that keep to these rules, and one draw needn't show every extreme that they name: `cache_len`: every device holds a request with exactly 512 cached tokens. The last 8 requests of a device continue from the device in the same gx row whose gy column is anchor, never from the device itself; one column sends at most 1 of them to one device, and some column sends exactly 1 to each device. `routes`: no expert is named by more than 48 of the rows of one device.
All inputs are finite; a program needn't handle non-finite values.
Results may differ from the reference program's by a relative error of at most 0.0038.
Values may be sent and summed in bfloat16 or wider, within the bound.
A program may use at most 192 MiB of HBM per device.

```python
import math
import jax
import jax.numpy as jnp
import numpy as np
from jax import lax

D = 1536
HEADS = 24
KV_HEADS = 8
HEAD = 64
EXPERTS = 32
FF = 512
TOP = 8
PAGE = 16
MAXLEN = 512
R_DEV = 16
P_DEV = 112
ROWS_DEV = 128
NPAGE = 32
LOCAL = 8
MOVED = 8
SLOT = 1
CAP = 48
POOL_DEV = 128
REQS = 2048
PREFILL = 14336
ROWS = 16384
N_GX = 8
N_GY = 16


def draw_queries(key, part):
    normal_noise = jax.random.normal(jax.random.fold_in(key, 1), (REQS, D), jnp.float32)
    values = jnp.clip(normal_noise, -6.0, 6.0)
    return values.astype(jnp.bfloat16)


def draw_cache_pool(key, part):
    page_count = REQS // R_DEV * POOL_DEV
    kv_width = 2 * KV_HEADS * HEAD
    dims_all = (page_count, PAGE, kv_width)
    values = jnp.clip(jax.random.normal(jax.random.fold_in(key, 3), dims_all, jnp.float32), -6.0, 6.0)
    return values.astype(jnp.bfloat16)


def draw_residual(key, part):
    normal_noise = jax.random.normal(jax.random.fold_in(key, 4), (ROWS, D), jnp.float32)
    values = jnp.clip(normal_noise, -6.0, 6.0)
    return values.astype(jnp.bfloat16)


def draw_router(key, part):
    normal_noise = jax.random.normal(jax.random.fold_in(key, 6), (D, EXPERTS), jnp.float32)
    values = jnp.clip(normal_noise, -6.0, 6.0) / math.sqrt(D)
    return values.astype(jnp.bfloat16)


def draw_cache_len(key, part):
    devices = REQS // R_DEV
    limits = jax.random.randint(jax.random.fold_in(key, 21), (devices, 1), MAXLEN // 4, MAXLEN + 1)
    raw_draw = jax.random.randint(jax.random.fold_in(key, 22), (devices, R_DEV), 0, MAXLEN)
    lengths = 1 + raw_draw * limits // MAXLEN
    longest = jax.random.randint(jax.random.fold_in(key, 23), (devices, 1), 0, R_DEV)
    lengths = jnp.where(jnp.arange(R_DEV)[None, :] == longest, MAXLEN, lengths)
    return lengths.reshape(REQS).astype(jnp.int32)


def draw_anchor(key, part):
    devices = REQS // R_DEV
    device_keys = jax.random.split(jax.random.fold_in(key, 31), devices)

    def one_device(device_key):
        first_key, second_key = jax.random.split(device_key)
        order_draw = jax.random.permutation(first_key, N_GY - 1) + 1
        offsets = jnp.tile(order_draw, SLOT)[:MOVED]
        return jax.random.permutation(second_key, offsets)
    offsets = jax.vmap(one_device)(device_keys)
    columns = jnp.arange(devices) % N_GY
    return ((columns[:, None] + offsets) % N_GY).reshape(devices * MOVED).astype(jnp.int32)


def set_ends(drawn, key, least, top_value):
    shape = drawn.shape
    spot = [jax.random.randint(jax.random.fold_in(key, axis), (), 0, shape[axis]) for axis in range(len(shape))]
    drawn = drawn.at[tuple(spot)].set(least)
    longest = shape.index(max(shape))
    spot[longest] = (spot[longest] + 1) % shape[longest]
    return drawn.at[tuple(spot)].set(top_value)


def steps_of(rng, extent, cuts, smallest, high):
    loudness, own = 1.0, jax.random.fold_in(rng, 6)
    for dim, blocks in cuts:
        draws = jnp.exp(jax.random.uniform(jax.random.fold_in(own, dim), (blocks,), jnp.float32, smallest / len(cuts), high / len(cuts)))
        loudness = loudness * jnp.repeat(draws, extent[dim] // blocks).reshape([-1 if axis == dim else 1 for axis in range(len(extent))])
    return loudness


def routed_block(rng, own, number, rows, amount, top, limit, skew):
    order = jax.random.permutation(rng, amount)
    heavy_load, common = shares(amount, rows * top, limit, skew, True), shares(amount, rows * top, limit, skew, False)
    places = jnp.arange(amount)

    def named(sizes, offset_by):
        used = int((sizes > 0).sum())
        fixed = max(1, used // 4)
        moved = fixed + (places - fixed + offset_by * (used - fixed)) % max(1, amount - fixed)
        return jnp.zeros((amount,), jnp.int32).at[order[jnp.where(places < fixed, places, moved)]].set(jnp.asarray(sizes, jnp.int32))

    sizes = jnp.where(number % 4 == 0, named(heavy_load, number // 4), named(common, number - number // 4 - 1))
    mixed = jax.random.permutation(jax.random.fold_in(own, 3), amount)
    giver, sink = mixed[0:amount // 2 * 2:2], mixed[1:amount // 2 * 2:2]
    margin = jnp.minimum(sizes[giver] - 1, limit - sizes[sink]) // 2
    margin = jnp.where((giver == order[0]) | (sink == order[0]) | (sizes[sink] == 0), 0, jnp.maximum(margin, 0))
    moved = jax.random.randint(jax.random.fold_in(own, 4), (amount // 2,), 0, 1 << 20) % (margin + 1)
    sizes = sizes.at[giver].add(-moved).at[sink].add(moved)
    members = jnp.searchsorted(jnp.cumsum(sizes), jnp.arange(rows * top), side="right").astype(jnp.int32)
    listing = members.reshape(top, rows).T
    listing = listing[jax.random.permutation(jax.random.fold_in(own, 1), rows)]
    offset_by = jax.random.randint(jax.random.fold_in(own, 2), (rows, 1), 0, top)
    return jnp.take_along_axis(listing, (jnp.arange(top)[None, :] + offset_by) % top, axis=1)


def shares(amount, total, reach, skew, full):
    loads = [(1 << 20) // math.isqrt(standing ** skew) + 1 for standing in range(1, amount + 1)]
    largest = reach if full else min(reach, max(-(-total // amount), total * loads[0] // sum(loads)))
    least = 1 if total - largest >= amount - 1 else 0
    given, rest = [largest] + [least] * (amount - 1), total - largest - least * (amount - 1)
    while rest > 0:
        movable = [i for i in range(1, amount) if given[i] < largest] or [i for i in range(1, amount) if given[i] < reach]
        whole, remaining = sum([loads[i] for i in movable]), rest
        for i in movable:
            extra = min(reach - given[i], max(1, remaining * loads[i] // whole), rest)
            given[i] = given[i] + extra
            rest = rest - extra
    return np.array(given)


def scatter_about(key, extent, deviation, limit, pieces=(), kind=jnp.bfloat16):
    factor_of = steps_of(key, extent, pieces, -0.22, 0.18) if pieces else 1.0
    result = jax.random.normal(key, extent, jnp.float32) * deviation * factor_of
    return jnp.minimum(jnp.maximum(result, -limit), limit).astype(kind)


def setup_inputs(seed: int = 0) -> dict:
    keys = jax.random.split(jax.random.key(seed), 16)
    queries = draw_queries(jax.random.fold_in(keys[15], 71), 0)
    new_kv = scatter_about(keys[1], (REQS, 2 * KV_HEADS * HEAD), 1.0, 6.0, ((0, 128),))
    cache_pool = draw_cache_pool(jax.random.fold_in(keys[15], 71), 0)
    cache_len = draw_cache_len(jax.random.fold_in(keys[15], 71), 0)
    local_pages = set_ends(jax.random.randint(keys[4], (REQS // R_DEV * LOCAL, NPAGE), 0, POOL_DEV), jax.random.fold_in(keys[4], 1), 0, POOL_DEV - 1).astype(jnp.int32)
    anchor = draw_anchor(jax.random.fold_in(keys[15], 71), 0)
    push_pages = set_ends(jax.random.randint(keys[6], (REQS // R_DEV * N_GY * SLOT, NPAGE), 0, POOL_DEV), jax.random.fold_in(keys[6], 1), 0, POOL_DEV - 1).astype(jnp.int32)
    prefill_attn = scatter_about(keys[7], (PREFILL, D), 0.5, 4.0, ((0, 128),))
    residual = draw_residual(jax.random.fold_in(keys[15], 71), 0)
    out_weight = scatter_about(keys[9], (D, D), D ** -0.5, 0.15625, ((0, 8),))
    norm_gain = jnp.clip(1.0 + 0.18 * jax.random.normal(keys[10], (D,), jnp.float32), 0.099609375, 1.8984375).astype(jnp.bfloat16)
    router = draw_router(jax.random.fold_in(keys[15], 71), 0)
    routes_keys = jax.random.split(jax.random.fold_in(keys[12], 1), ROWS // ROWS_DEV)
    routes_turns = jax.random.permutation(jax.random.fold_in(keys[12], 3), ROWS // ROWS_DEV)
    routes = jax.vmap(lambda own, number: routed_block(jax.random.fold_in(keys[12], 2), own, number, ROWS_DEV, EXPERTS, TOP, CAP, 2))(routes_keys, routes_turns).reshape((ROWS, TOP))
    gate_up = scatter_about(keys[13], (D, EXPERTS, 2 * FF), D ** -0.5, 0.15625, ((0, 8), (1, 16)))
    down_proj = scatter_about(keys[14], (D, EXPERTS, FF), FF ** -0.5, 0.25, ((0, 8), (1, 16)))
    return {"queries": queries, "new_kv": new_kv, "cache_pool": cache_pool, "cache_len": cache_len, "local_pages": local_pages, "anchor": anchor, "push_pages": push_pages, "prefill_attn": prefill_attn, "residual": residual, "out_weight": out_weight, "norm_gain": norm_gain, "router": router, "routes": routes, "gate_up": gate_up, "down_proj": down_proj}


def partial_attend(query_heads, keyval, lengths):
    count_req, positions, kv_width = keyval.shape
    kv_count = query_heads.shape[1]
    head_size = query_heads.shape[3]
    half_width = kv_count * head_size
    key_rows = keyval[:, :, :half_width].reshape(count_req, positions, kv_count, head_size)
    value_rows = keyval[:, :, half_width:].reshape(count_req, positions, kv_count, head_size)
    scores = jnp.einsum('nkgh,ntkh->nkgt', query_heads.astype(jnp.float32), key_rows.astype(jnp.float32)) * (1.0 / math.sqrt(head_size))
    valid = (jnp.arange(positions)[None, :] < lengths[:, None])[:, None, None, :]
    masked = jnp.where(valid, scores, -1e+30)
    cache_max = lax.optimization_barrier(jnp.max(masked, axis=3))
    expos = jnp.where(valid, jnp.exp(masked - cache_max[..., None]), 0.0)
    totals = lax.optimization_barrier(jnp.sum(expos, axis=3))
    weights = lax.optimization_barrier(expos.astype(jnp.bfloat16)).astype(jnp.float32)
    mixture = jnp.einsum('nkgt,ntkh->nkgh', weights, value_rows.astype(jnp.float32))
    return (cache_max, totals, mixture)

def finish(query_heads, fresh, cache_max, totals, mixture):
    count_req, kv_count, group_size, head_size = query_heads.shape
    half_width = kv_count * head_size
    own_key = fresh[:, :half_width].reshape(count_req, kv_count, head_size)
    own_value = fresh[:, half_width:].reshape(count_req, kv_count, head_size).astype(jnp.float32)
    own_score = jnp.einsum('nkgh,nkh->nkg', query_heads.astype(jnp.float32), own_key.astype(jnp.float32)) * (1.0 / math.sqrt(head_size))
    highest = jnp.maximum(cache_max, own_score)
    old_share = jnp.exp(cache_max - highest)
    new_share = jnp.exp(own_score - highest)
    weighted = old_share[..., None] * mixture + new_share[..., None] * own_value[:, :, None, :]
    output = weighted / (old_share * totals + new_share)[..., None]
    return output.reshape(count_req, kv_count * group_size * head_size).astype(jnp.bfloat16)

def reference(queries, new_kv, cache_pool, cache_len, local_pages, anchor, push_pages, prefill_attn, residual, out_weight, norm_gain, router, routes, gate_up, down_proj):
    devices = N_GX * N_GY
    group_size = HEADS // KV_HEADS
    kv_width = 2 * KV_HEADS * HEAD
    pool_all = cache_pool.reshape(devices, POOL_DEV, PAGE, kv_width)
    local_all = local_pages.reshape(devices, LOCAL, NPAGE)
    anchor_all = anchor.reshape(devices, MOVED)
    push_all = push_pages.reshape(devices, N_GY, SLOT, NPAGE)
    matches = (anchor_all[:, :, None] == jnp.arange(N_GY, dtype=jnp.int32)[None, None, :]).astype(jnp.int32)
    earlier = lax.optimization_barrier(jnp.sum((jnp.cumsum(matches, axis=1) - 1) * matches, axis=2)).astype(jnp.int32)
    query_all = queries.reshape(devices, R_DEV, KV_HEADS, group_size, HEAD)
    length_all = cache_len.reshape(devices, R_DEV)
    fresh_all = new_kv.reshape(devices, R_DEV, kv_width)

    def attend_device(device_index):
        gx_row = device_index // N_GY
        gy_column = device_index % N_GY
        own_pool = pool_all[device_index]
        local_kv = own_pool[local_all[device_index]].reshape(LOCAL, MAXLEN, kv_width)
        sources = (gx_row * N_GY + anchor_all[device_index]).astype(jnp.int32)
        page_ids = push_all[sources, gy_column, earlier[device_index]]
        moved_kv = pool_all[sources[:, None], page_ids].reshape(MOVED, MAXLEN, kv_width)
        keyval = jnp.concatenate([local_kv, moved_kv], axis=0)
        cache_max, totals, mixture = partial_attend(query_all[device_index], keyval, length_all[device_index])
        return finish(query_all[device_index], fresh_all[device_index], cache_max, totals, mixture)
    attended = lax.map(attend_device, jnp.arange(devices, dtype=jnp.int32)).reshape(REQS, D)
    tokens = jnp.concatenate([attended.reshape(devices, R_DEV, D), prefill_attn.reshape(devices, P_DEV, D)], axis=1).reshape(ROWS, D)
    stream = residual.astype(jnp.float32) + jnp.dot(tokens, out_weight, preferred_element_type=jnp.float32)
    normed = (stream * lax.rsqrt(lax.optimization_barrier(jnp.mean(stream * stream, axis=1, keepdims=True)) + 1e-06) * norm_gain.astype(jnp.float32)).astype(jnp.bfloat16)
    logits = jnp.dot(normed, router, preferred_element_type=jnp.float32)
    chosen_logits = jnp.take_along_axis(logits, routes, axis=1)
    gate_weights = jax.nn.softmax(chosen_logits, axis=1)
    pair_weights = jnp.transpose(gate_up, (1, 0, 2)).astype(jnp.float32)
    down_weights = jnp.transpose(down_proj, (1, 2, 0)).astype(jnp.float32)
    normed_all = normed.reshape(devices, ROWS_DEV, D)
    routes_all = routes.reshape(devices, ROWS_DEV * TOP)
    gates_all = gate_weights.reshape(devices, ROWS_DEV, TOP)

    def experts_device(device_index):
        routes_dev = routes_all[device_index]
        route_hits = (routes_dev[:, None] == jnp.arange(EXPERTS, dtype=jnp.int32)[None, :]).astype(jnp.int32)
        places = lax.optimization_barrier(jnp.sum((jnp.cumsum(route_hits, axis=0) - 1) * route_hits, axis=1)).astype(jnp.int32)
        targets = (routes_dev * CAP + places).astype(jnp.int32)
        repeated = jnp.repeat(normed_all[device_index], TOP, axis=0)
        slab = jnp.zeros((EXPERTS * CAP, D), jnp.bfloat16).at[targets].set(repeated).reshape(EXPERTS, CAP, D)
        gate_pair = jnp.einsum('ecd,edf->ecf', slab.astype(jnp.float32), pair_weights)
        hidden = (jax.nn.silu(gate_pair[..., :FF]) * gate_pair[..., FF:]).astype(jnp.bfloat16)
        expert_rows = jnp.einsum('ecf,efd->ecd', hidden.astype(jnp.float32), down_weights).astype(jnp.bfloat16)
        picked = expert_rows.reshape(EXPERTS * CAP, D)[targets]
        picked = lax.optimization_barrier(picked).astype(jnp.float32).reshape(ROWS_DEV, TOP, D)
        return lax.optimization_barrier(jnp.sum(gates_all[device_index][:, :, None] * picked, axis=1))
    mixed = lax.map(experts_device, jnp.arange(devices, dtype=jnp.int32)).reshape(ROWS, D)
    layer_out = stream + mixed
    return (attended, layer_out)
```

```python
import math

import jax
import jax.numpy as jnp
from jax import lax
from jax.sharding import PartitionSpec as P
from jax.experimental import pallas as pl
from jax.experimental.pallas import tpu as pltpu

D = 1536
HEADS = 24
KV_HEADS = 8
HEAD = 64
EXPERTS = 32
FF = 512
TOP = 8
MAXLEN = 512
R_DEV = 16
LOCAL = 8
MOVED = 8
CAP = 48
NPAGE = 32
PAGE = 16


def attend_kernel(tables, lengths, q_ref, pool_ref, max_ref, tot_ref, mix_ref, kvbuf, sems):
    r = pl.program_id(0)
    n = pl.num_programs(0)
    half = KV_HEADS * HEAD

    def start(req, slot):
        def one(p, carry):
            pltpu.make_async_copy(
                pool_ref.at[tables[req, p]], kvbuf.at[slot, p], sems.at[slot]
            ).start()
            return carry

        lax.fori_loop(0, NPAGE, one, 0, unroll=8)

    @pl.when(r == 0)
    def _():
        start(0, 0)

    slot = r % 2

    @pl.when(r + 1 < n)
    def _():
        start(r + 1, 1 - slot)

    pltpu.make_async_copy(pool_ref.at[pl.ds(0, NPAGE)], kvbuf.at[slot], sems.at[slot]).wait()
    kv = kvbuf.at[slot]
    keys = kv[:, :, :half].reshape(MAXLEN, half)
    values = kv[:, :, half:].reshape(MAXLEN, half)
    q = q_ref[0]
    scores = lax.dot_general(
        q, keys, (((1,), (1,)), ((), ())), preferred_element_type=jnp.float32
    ) * (1.0 / math.sqrt(HEAD))
    valid = lax.broadcasted_iota(jnp.int32, scores.shape, 1) < lengths[r]
    masked = jnp.where(valid, scores, -1e30)
    top = jnp.max(masked, axis=1, keepdims=True)
    expos = jnp.where(valid, jnp.exp(masked - top), 0.0)
    total = jnp.sum(expos, axis=1, keepdims=True)
    mix = jnp.dot(expos.astype(jnp.bfloat16), values, preferred_element_type=jnp.float32)
    max_ref[0] = jnp.broadcast_to(top, max_ref.shape[1:])
    tot_ref[0] = jnp.broadcast_to(total, tot_ref.shape[1:])
    mix_ref[0] = mix


def paged_attend(query_rows, tables, lengths, pool):
    count = query_rows.shape[0]
    group_size = HEADS // KV_HEADS
    half = KV_HEADS * HEAD
    heads = query_rows.reshape(count, KV_HEADS, group_size, 1, HEAD)
    mask = (jnp.arange(KV_HEADS)[:, None] == jnp.arange(KV_HEADS)[None, :])
    spread = jnp.where(
        mask[None, :, None, :, None], heads, jnp.zeros((), query_rows.dtype)
    ).reshape(count, HEADS, half)
    kv_width = pool.shape[2]
    grid_spec = pltpu.PrefetchScalarGridSpec(
        num_scalar_prefetch=2,
        grid=(count,),
        in_specs=[
            pl.BlockSpec((1, HEADS, half), lambda r, t, l: (r, 0, 0)),
            pl.BlockSpec(memory_space=pl.ANY),
        ],
        out_specs=[
            pl.BlockSpec((1, HEADS, 128), lambda r, t, l: (r, 0, 0)),
            pl.BlockSpec((1, HEADS, 128), lambda r, t, l: (r, 0, 0)),
            pl.BlockSpec((1, HEADS, half), lambda r, t, l: (r, 0, 0)),
        ],
        scratch_shapes=[
            pltpu.VMEM((2, NPAGE, PAGE, kv_width), pool.dtype),
            pltpu.SemaphoreType.DMA((2,)),
        ],
    )
    top, total, mix = pl.pallas_call(
        attend_kernel,
        grid_spec=grid_spec,
        out_shape=[
            jax.ShapeDtypeStruct((count, HEADS, 128), jnp.float32),
            jax.ShapeDtypeStruct((count, HEADS, 128), jnp.float32),
            jax.ShapeDtypeStruct((count, HEADS, half), jnp.float32),
        ],
        compiler_params=pltpu.CompilerParams(dimension_semantics=("arbitrary",)),
        cost_estimate=pl.CostEstimate(
            flops=count * 4 * HEADS * MAXLEN * half,
            transcendentals=count * HEADS * MAXLEN,
            bytes_accessed=count * MAXLEN * kv_width * 2,
        ),
    )(tables, lengths, spread, pool)
    blocks = mix.reshape(count, KV_HEADS, group_size, KV_HEADS, HEAD)
    mixture = jnp.sum(jnp.where(mask[None, :, None, :, None], blocks, 0.0), axis=3)
    return (
        top[:, :, 0].reshape(count, KV_HEADS, group_size),
        total[:, :, 0].reshape(count, KV_HEADS, group_size),
        mixture,
    )


def in_one_piece(arrays, axis, split_dim, concat_dim, along):
    columns = [a.reshape(*a.shape[:along], -1) for a in arrays]
    both = jnp.concatenate(columns, axis=along)
    result, at, gathered = (
        lax.all_to_all(both, axis, split_axis=split_dim, concat_axis=concat_dim, tiled=True),
        0,
        [],
    )
    for a, column in zip(arrays, columns):
        share = result[..., at : at + column.shape[along]]
        gathered.append(share.reshape(*share.shape[:along], *a.shape[along:]))
        at += column.shape[along]
    return tuple(gathered)


def side_by_side(arrays, axis, dim, along):
    widths = [math.prod(a.shape[along:]) for a in arrays]
    both = jnp.concatenate(
        [a.reshape(*a.shape[:along], w) for a, w in zip(arrays, widths)], axis=along
    )
    result = lax.all_gather(both, axis, axis=dim, tiled=True)
    blocks = jnp.split(result, [sum(widths[:k]) for k in range(1, len(widths))], axis=along)
    return tuple(
        (b.reshape(*result.shape[:along], *a.shape[along:]) for a, b in zip(arrays, blocks))
    )


def partial_attend(query_heads, keyval, lengths):
    count_req, positions, kv_width = keyval.shape
    kv_count = query_heads.shape[1]
    head_size = query_heads.shape[3]
    half_width = kv_count * head_size
    key_rows = keyval[:, :, :half_width].reshape(count_req, positions, kv_count, head_size)
    value_rows = keyval[:, :, half_width:].reshape(count_req, positions, kv_count, head_size)
    scores = jnp.einsum(
        "nkgh,ntkh->nkgt", query_heads, key_rows, preferred_element_type=jnp.float32
    ) * (1.0 / math.sqrt(head_size))
    valid = (jnp.arange(positions)[None, :] < lengths[:, None])[:, None, None, :]
    masked = jnp.where(valid, scores, -1e30)
    cache_max = jnp.max(masked, axis=3)
    expos = jnp.where(valid, jnp.exp(masked - cache_max[..., None]), 0.0)
    totals = jnp.sum(expos, axis=3)
    weights = expos.astype(jnp.bfloat16)
    mixture = jnp.einsum("nkgt,ntkh->nkgh", weights, value_rows, preferred_element_type=jnp.float32)
    return (cache_max, totals, mixture)


def finish(query_heads, fresh, cache_max, totals, mixture):
    count_req, kv_count, group_size, head_size = query_heads.shape
    half_width = kv_count * head_size
    own_key = fresh[:, :half_width].reshape(count_req, kv_count, head_size)
    own_value = fresh[:, half_width:].reshape(count_req, kv_count, head_size).astype(jnp.float32)
    own_score = jnp.einsum(
        "nkgh,nkh->nkg", query_heads, own_key, preferred_element_type=jnp.float32
    ) * (1.0 / math.sqrt(head_size))
    highest = jnp.maximum(cache_max, own_score)
    old_share = jnp.exp(cache_max - highest)
    new_share = jnp.exp(own_score - highest)
    weighted = old_share[..., None] * mixture + new_share[..., None] * own_value[:, :, None, :]
    output = weighted / (old_share * totals + new_share)[..., None]
    return output.reshape(count_req, kv_count * group_size * head_size).astype(jnp.bfloat16)


def body(
    queries,
    new_kv,
    cache_pool,
    cache_len,
    local_pages,
    anchor,
    push_pages,
    prefill_attn,
    residual,
    out_weight,
    norm_gain,
    router,
    routes,
    gate_up,
    down_proj,
):
    columns = lax.axis_size("gy")
    slot_count = (MOVED + columns - 2) // (columns - 1)
    group_size = HEADS // KV_HEADS
    kv_width = 2 * KV_HEADS * HEAD
    query_heads = queries.reshape(R_DEV, KV_HEADS, group_size, HEAD)
    matches = (anchor[:, None] == jnp.arange(columns, dtype=jnp.int32)[None, :]).astype(jnp.int32)
    earlier = jnp.sum((jnp.cumsum(matches, axis=0) - 1) * matches, axis=1)
    chosen = anchor * slot_count + earlier
    local_max, local_totals, local_mix = paged_attend(
        queries[:LOCAL], local_pages, cache_len[:LOCAL], cache_pool
    )
    picker = chosen[:, None] == jnp.arange(columns * slot_count, dtype=jnp.int32)[None, :]
    sent_queries = jnp.einsum(
        "ms,md->sd",
        picker.astype(jnp.bfloat16),
        queries[LOCAL:],
        preferred_element_type=jnp.float32,
    )
    sent_lengths = jnp.sum(
        jnp.where(picker, cache_len[LOCAL:, None].astype(jnp.float32), 0.0), axis=0
    )
    got_queries, got_lengths = in_one_piece(
        (sent_queries.reshape(columns, slot_count, D), sent_lengths.reshape(columns, slot_count)),
        "gy",
        0,
        0,
        2,
    )
    far_max, far_totals, far_mix = paged_attend(
        got_queries.astype(jnp.bfloat16).reshape(columns * slot_count, D),
        push_pages,
        got_lengths.reshape(columns * slot_count).astype(jnp.int32),
        cache_pool,
    )
    back_max, back_totals, back_mix = in_one_piece(
        (
            far_max.reshape(columns, slot_count, KV_HEADS, group_size),
            far_totals.reshape(columns, slot_count, KV_HEADS, group_size),
            far_mix.reshape(columns, slot_count, KV_HEADS, group_size, HEAD),
        ),
        "gy",
        0,
        0,
        4,
    )
    cache_max = jnp.concatenate(
        [local_max, back_max.reshape(columns * slot_count, KV_HEADS, group_size)[chosen]], axis=0
    )
    totals = jnp.concatenate(
        [local_totals, back_totals.reshape(columns * slot_count, KV_HEADS, group_size)[chosen]],
        axis=0,
    )
    mixture = jnp.concatenate(
        [local_mix, back_mix.reshape(columns * slot_count, KV_HEADS, group_size, HEAD)[chosen]],
        axis=0,
    )
    attended = finish(query_heads, new_kv, cache_max, totals, mixture)
    tokens = jnp.concatenate([attended, prefill_attn], axis=0)
    row_count = tokens.shape[0]
    full_out, full_pair, full_down = side_by_side((out_weight, gate_up, down_proj), "gx", 0, 1)
    stream = residual.astype(jnp.float32) + jnp.dot(
        tokens, full_out, preferred_element_type=jnp.float32
    )
    normed = (
        stream
        * lax.rsqrt(jnp.mean(stream * stream, axis=1, keepdims=True) + 1e-06)
        * norm_gain.astype(jnp.float32)
    ).astype(jnp.bfloat16)
    logits = jnp.dot(normed, router, preferred_element_type=jnp.float32)
    selector = routes[:, :, None] == jnp.arange(EXPERTS, dtype=jnp.int32)[None, None, :]
    gate_weights = jax.nn.softmax(
        jnp.sum(jnp.where(selector, logits[:, None, :], 0.0), axis=2), axis=1
    )
    flat_routes = routes.reshape(row_count * TOP)
    route_hits = (flat_routes[:, None] == jnp.arange(EXPERTS, dtype=jnp.int32)[None, :]).astype(
        jnp.int32
    )
    places = jnp.sum((jnp.cumsum(route_hits, axis=0) - 1) * route_hits, axis=1)
    targets = flat_routes * CAP + places
    repeated = jnp.repeat(normed, TOP, axis=0)
    experts_dev = full_pair.shape[1]
    outgoing_rows = (
        jnp.zeros((EXPERTS * CAP, D), jnp.bfloat16)
        .at[targets]
        .set(repeated)
        .reshape(columns, experts_dev, CAP, D)
    )
    arrived = lax.all_to_all(outgoing_rows, "gy", split_axis=0, concat_axis=0, tiled=True)
    gate_pair = jnp.einsum("secd,def->secf", arrived, full_pair, preferred_element_type=jnp.float32)
    hidden = (jax.nn.silu(gate_pair[..., :FF]) * gate_pair[..., FF:]).astype(jnp.bfloat16)
    expert_rows = jnp.einsum(
        "secf,def->secd", hidden, full_down, preferred_element_type=jnp.float32
    ).astype(jnp.bfloat16)
    returned = lax.all_to_all(expert_rows, "gy", split_axis=0, concat_axis=0, tiled=True).reshape(
        EXPERTS * CAP, D
    )
    picked = returned[targets].astype(jnp.float32).reshape(row_count, TOP, D)
    layer_out = stream + jnp.sum(gate_weights[:, :, None] * picked, axis=1)
    return (attended, layer_out)


def solution(mesh):
    placed = (
        P(("gx", "gy"), None),
        P(("gx", "gy"), None),
        P(("gx", "gy"), None, None),
        P(("gx", "gy")),
        P(("gx", "gy"), None),
        P(("gx", "gy")),
        P(("gx", "gy"), None),
        P(("gx", "gy"), None),
        P(("gx", "gy"), None),
        P("gx", None),
        P(),
        P(),
        P(("gx", "gy"), None),
        P("gx", "gy", None),
        P("gx", "gy", None),
    )
    return jax.shard_map(
        body,
        mesh=mesh,
        in_specs=placed,
        out_specs=(P(("gx", "gy"), None), P(("gx", "gy"), None)),
        check_vma=False,
    )
```

```python
import math

import jax
import jax.numpy as jnp
from jax import lax
from jax.sharding import PartitionSpec as P
from jax.experimental import pallas as pl
from jax.experimental.pallas import tpu as pltpu

D = 1536
HEADS = 24
KV_HEADS = 8
HEAD = 64
EXPERTS = 32
FF = 512
TOP = 8
MAXLEN = 512
R_DEV = 16
LOCAL = 8
MOVED = 8
CAP = 48
NPAGE = 32
PAGE = 16


def attend_kernel(tables, lengths, q_ref, pool_ref, max_ref, tot_ref, mix_ref, kvbuf, sems):
    r = pl.program_id(0)
    n = pl.num_programs(0)
    half = KV_HEADS * HEAD

    def start(req, slot):
        def one(p, carry):
            pltpu.make_async_copy(
                pool_ref.at[tables[req, p]], kvbuf.at[slot, p], sems.at[slot]
            ).start()
            return carry

        lax.fori_loop(0, NPAGE, one, 0, unroll=8)

    @pl.when(r == 0)
    def _():
        start(0, 0)

    slot = r % 2

    @pl.when(r + 1 < n)
    def _():
        start(r + 1, 1 - slot)

    pltpu.make_async_copy(pool_ref.at[pl.ds(0, NPAGE)], kvbuf.at[slot], sems.at[slot]).wait()
    kv = kvbuf.at[slot]
    keys = kv[:, :, :half].reshape(MAXLEN, half)
    values = kv[:, :, half:].reshape(MAXLEN, half)
    q = q_ref[0]
    scores = lax.dot_general(
        q, keys, (((1,), (1,)), ((), ())), preferred_element_type=jnp.float32
    ) * (1.0 / math.sqrt(HEAD))
    valid = lax.broadcasted_iota(jnp.int32, scores.shape, 1) < lengths[r]
    masked = jnp.where(valid, scores, -1e30)
    top = jnp.max(masked, axis=1, keepdims=True)
    expos = jnp.where(valid, jnp.exp(masked - top), 0.0)
    total = jnp.sum(expos, axis=1, keepdims=True)
    mix = jnp.dot(expos.astype(jnp.bfloat16), values, preferred_element_type=jnp.float32)
    max_ref[0] = jnp.broadcast_to(top, max_ref.shape[1:])
    tot_ref[0] = jnp.broadcast_to(total, tot_ref.shape[1:])
    mix_ref[0] = mix


def paged_attend(query_rows, tables, lengths, pool):
    count = query_rows.shape[0]
    group_size = HEADS // KV_HEADS
    half = KV_HEADS * HEAD
    heads = query_rows.reshape(count, KV_HEADS, group_size, 1, HEAD)
    mask = (jnp.arange(KV_HEADS)[:, None] == jnp.arange(KV_HEADS)[None, :])
    spread = jnp.where(
        mask[None, :, None, :, None], heads, jnp.zeros((), query_rows.dtype)
    ).reshape(count, HEADS, half)
    kv_width = pool.shape[2]
    grid_spec = pltpu.PrefetchScalarGridSpec(
        num_scalar_prefetch=2,
        grid=(count,),
        in_specs=[
            pl.BlockSpec((1, HEADS, half), lambda r, t, l: (r, 0, 0)),
            pl.BlockSpec(memory_space=pl.ANY),
        ],
        out_specs=[
            pl.BlockSpec((1, HEADS, 128), lambda r, t, l: (r, 0, 0)),
            pl.BlockSpec((1, HEADS, 128), lambda r, t, l: (r, 0, 0)),
            pl.BlockSpec((1, HEADS, half), lambda r, t, l: (r, 0, 0)),
        ],
        scratch_shapes=[
            pltpu.VMEM((2, NPAGE, PAGE, kv_width), pool.dtype),
            pltpu.SemaphoreType.DMA((2,)),
        ],
    )
    top, total, mix = pl.pallas_call(
        attend_kernel,
        grid_spec=grid_spec,
        out_shape=[
            jax.ShapeDtypeStruct((count, HEADS, 128), jnp.float32),
            jax.ShapeDtypeStruct((count, HEADS, 128), jnp.float32),
            jax.ShapeDtypeStruct((count, HEADS, half), jnp.float32),
        ],
        compiler_params=pltpu.CompilerParams(dimension_semantics=("arbitrary",)),
        cost_estimate=pl.CostEstimate(
            flops=count * 4 * HEADS * MAXLEN * half,
            transcendentals=count * HEADS * MAXLEN,
            bytes_accessed=count * MAXLEN * kv_width * 2,
        ),
    )(tables, lengths, spread, pool)
    blocks = mix.reshape(count, KV_HEADS, group_size, KV_HEADS, HEAD)
    mixture = jnp.sum(jnp.where(mask[None, :, None, :, None], blocks, 0.0), axis=3)
    return (
        top[:, :, 0].reshape(count, KV_HEADS, group_size),
        total[:, :, 0].reshape(count, KV_HEADS, group_size),
        mixture,
    )


def in_one_piece(arrays, axis, split_dim, concat_dim, along):
    columns = [a.reshape(*a.shape[:along], -1) for a in arrays]
    both = jnp.concatenate(columns, axis=along)
    result, at, gathered = (
        lax.all_to_all(both, axis, split_axis=split_dim, concat_axis=concat_dim, tiled=True),
        0,
        [],
    )
    for a, column in zip(arrays, columns):
        share = result[..., at : at + column.shape[along]]
        gathered.append(share.reshape(*share.shape[:along], *a.shape[along:]))
        at += column.shape[along]
    return tuple(gathered)


def side_by_side(arrays, axis, dim, along):
    widths = [math.prod(a.shape[along:]) for a in arrays]
    both = jnp.concatenate(
        [a.reshape(*a.shape[:along], w) for a, w in zip(arrays, widths)], axis=along
    )
    result = lax.all_gather(both, axis, axis=dim, tiled=True)
    blocks = jnp.split(result, [sum(widths[:k]) for k in range(1, len(widths))], axis=along)
    return tuple(
        (b.reshape(*result.shape[:along], *a.shape[along:]) for a, b in zip(arrays, blocks))
    )


def partial_attend(query_heads, keyval, lengths):
    count_req, positions, kv_width = keyval.shape
    kv_count = query_heads.shape[1]
    head_size = query_heads.shape[3]
    half_width = kv_count * head_size
    key_rows = keyval[:, :, :half_width].reshape(count_req, positions, kv_count, head_size)
    value_rows = keyval[:, :, half_width:].reshape(count_req, positions, kv_count, head_size)
    scores = jnp.einsum(
        "nkgh,ntkh->nkgt", query_heads, key_rows, preferred_element_type=jnp.float32
    ) * (1.0 / math.sqrt(head_size))
    valid = (jnp.arange(positions)[None, :] < lengths[:, None])[:, None, None, :]
    masked = jnp.where(valid, scores, -1e30)
    cache_max = jnp.max(masked, axis=3)
    expos = jnp.where(valid, jnp.exp(masked - cache_max[..., None]), 0.0)
    totals = jnp.sum(expos, axis=3)
    weights = expos.astype(jnp.bfloat16)
    mixture = jnp.einsum("nkgt,ntkh->nkgh", weights, value_rows, preferred_element_type=jnp.float32)
    return (cache_max, totals, mixture)


def finish(query_heads, fresh, cache_max, totals, mixture):
    count_req, kv_count, group_size, head_size = query_heads.shape
    half_width = kv_count * head_size
    own_key = fresh[:, :half_width].reshape(count_req, kv_count, head_size)
    own_value = fresh[:, half_width:].reshape(count_req, kv_count, head_size).astype(jnp.float32)
    own_score = jnp.einsum(
        "nkgh,nkh->nkg", query_heads, own_key, preferred_element_type=jnp.float32
    ) * (1.0 / math.sqrt(head_size))
    highest = jnp.maximum(cache_max, own_score)
    old_share = jnp.exp(cache_max - highest)
    new_share = jnp.exp(own_score - highest)
    weighted = old_share[..., None] * mixture + new_share[..., None] * own_value[:, :, None, :]
    output = weighted / (old_share * totals + new_share)[..., None]
    return output.reshape(count_req, kv_count * group_size * head_size).astype(jnp.bfloat16)


def body(
    queries,
    new_kv,
    cache_pool,
    cache_len,
    local_pages,
    anchor,
    push_pages,
    prefill_attn,
    residual,
    out_weight,
    norm_gain,
    router,
    routes,
    gate_up,
    down_proj,
):
    columns = lax.axis_size("gy")
    slot_count = (MOVED + columns - 2) // (columns - 1)
    group_size = HEADS // KV_HEADS
    kv_width = 2 * KV_HEADS * HEAD
    query_heads = queries.reshape(R_DEV, KV_HEADS, group_size, HEAD)
    matches = (anchor[:, None] == jnp.arange(columns, dtype=jnp.int32)[None, :]).astype(jnp.int32)
    earlier = jnp.sum((jnp.cumsum(matches, axis=0) - 1) * matches, axis=1)
    chosen = anchor * slot_count + earlier
    local_max, local_totals, local_mix = paged_attend(
        queries[:LOCAL], local_pages, cache_len[:LOCAL], cache_pool
    )
    picker = chosen[:, None] == jnp.arange(columns * slot_count, dtype=jnp.int32)[None, :]
    sent_queries = jnp.einsum(
        "ms,md->sd",
        picker.astype(jnp.bfloat16),
        queries[LOCAL:],
        preferred_element_type=jnp.float32,
    )
    sent_lengths = jnp.sum(
        jnp.where(picker, cache_len[LOCAL:, None].astype(jnp.float32), 0.0), axis=0
    )
    got_queries, got_lengths = in_one_piece(
        (sent_queries.reshape(columns, slot_count, D), sent_lengths.reshape(columns, slot_count)),
        "gy",
        0,
        0,
        2,
    )
    far_max, far_totals, far_mix = paged_attend(
        got_queries.astype(jnp.bfloat16).reshape(columns * slot_count, D),
        push_pages,
        got_lengths.reshape(columns * slot_count).astype(jnp.int32),
        cache_pool,
    )
    back_max, back_totals, back_mix = in_one_piece(
        (
            far_max.reshape(columns, slot_count, KV_HEADS, group_size),
            far_totals.reshape(columns, slot_count, KV_HEADS, group_size),
            far_mix.reshape(columns, slot_count, KV_HEADS, group_size, HEAD),
        ),
        "gy",
        0,
        0,
        4,
    )
    cache_max = jnp.concatenate(
        [local_max, back_max.reshape(columns * slot_count, KV_HEADS, group_size)[chosen]], axis=0
    )
    totals = jnp.concatenate(
        [local_totals, back_totals.reshape(columns * slot_count, KV_HEADS, group_size)[chosen]],
        axis=0,
    )
    mixture = jnp.concatenate(
        [local_mix, back_mix.reshape(columns * slot_count, KV_HEADS, group_size, HEAD)[chosen]],
        axis=0,
    )
    attended = finish(query_heads, new_kv, cache_max, totals, mixture)
    tokens = jnp.concatenate([attended, prefill_attn], axis=0)
    row_count = tokens.shape[0]
    full_out = lax.all_gather(out_weight, "gx", axis=0, tiled=True)
    full_pair = lax.all_gather(gate_up, "gx", axis=0, tiled=True)
    full_down = lax.all_gather(down_proj, "gx", axis=0, tiled=True)
    stream = residual.astype(jnp.float32) + jnp.dot(
        tokens, full_out, preferred_element_type=jnp.float32
    )
    normed = (
        stream
        * lax.rsqrt(jnp.mean(stream * stream, axis=1, keepdims=True) + 1e-06)
        * norm_gain.astype(jnp.float32)
    ).astype(jnp.bfloat16)
    logits = jnp.dot(normed, router, preferred_element_type=jnp.float32)
    selector = routes[:, :, None] == jnp.arange(EXPERTS, dtype=jnp.int32)[None, None, :]
    gate_weights = jax.nn.softmax(
        jnp.sum(jnp.where(selector, logits[:, None, :], 0.0), axis=2), axis=1
    )
    dense_gates = jnp.where(
        jnp.any(selector, axis=1),
        jnp.sum(jnp.where(selector, gate_weights[:, :, None], 0.0), axis=1),
        -1.0,
    )
    experts_dev = full_pair.shape[1]
    all_normed = lax.all_gather(normed, "gy", axis=0, tiled=True)
    all_gates = lax.all_gather(dense_gates, "gy", axis=0, tiled=True)
    first = lax.axis_index("gy") * experts_dev
    my_gates = lax.dynamic_slice_in_dim(all_gates, first, experts_dev, axis=1)
    my_routed = my_gates >= 0.0
    gate_pair = jnp.einsum("rd,def->ref", all_normed, full_pair, preferred_element_type=jnp.float32)
    hidden = (jax.nn.silu(gate_pair[..., :FF]) * gate_pair[..., FF:]).astype(jnp.bfloat16)
    expert_rows = jnp.einsum(
        "ref,def->red", hidden, full_down, preferred_element_type=jnp.float32
    ).astype(jnp.bfloat16)
    partial = jnp.sum(
        jnp.where(my_routed[..., None], my_gates[..., None] * expert_rows.astype(jnp.float32), 0.0),
        axis=1,
    )
    mixed = lax.psum_scatter(partial, "gy", scatter_dimension=0, tiled=True)
    layer_out = stream + mixed
    return (attended, layer_out)


def solution(mesh):
    placed = (
        P(("gx", "gy"), None),
        P(("gx", "gy"), None),
        P(("gx", "gy"), None, None),
        P(("gx", "gy")),
        P(("gx", "gy"), None),
        P(("gx", "gy")),
        P(("gx", "gy"), None),
        P(("gx", "gy"), None),
        P(("gx", "gy"), None),
        P("gx", None),
        P(),
        P(),
        P(("gx", "gy"), None),
        P("gx", "gy", None),
        P("gx", "gy", None),
    )
    return jax.shard_map(
        body,
        mesh=mesh,
        in_specs=placed,
        out_specs=(P(("gx", "gy"), None), P(("gx", "gy"), None)),
        check_vma=False,
    )
```

```python
import math

import jax
import jax.numpy as jnp
from jax import lax
from jax.sharding import PartitionSpec as P
from jax.experimental import pallas as pl
from jax.experimental.pallas import tpu as pltpu

D = 1536
HEADS = 24
KV_HEADS = 8
HEAD = 64
EXPERTS = 32
FF = 512
TOP = 8
MAXLEN = 512
R_DEV = 16
LOCAL = 8
MOVED = 8
CAP = 48
NPAGE = 32
PAGE = 16


def attend_kernel(tables, lengths, q_ref, pool_ref, max_ref, tot_ref, mix_ref, kvbuf, sems):
    r = pl.program_id(0)
    n = pl.num_programs(0)
    half = KV_HEADS * HEAD

    def start(req, slot):
        def one(p, carry):
            pltpu.make_async_copy(
                pool_ref.at[tables[req, p]], kvbuf.at[slot, p], sems.at[slot]
            ).start()
            return carry

        lax.fori_loop(0, NPAGE, one, 0, unroll=8)

    @pl.when(r == 0)
    def _():
        start(0, 0)

    slot = r % 2

    @pl.when(r + 1 < n)
    def _():
        start(r + 1, 1 - slot)

    pltpu.make_async_copy(pool_ref.at[pl.ds(0, NPAGE)], kvbuf.at[slot], sems.at[slot]).wait()
    kv = kvbuf.at[slot]
    keys = kv[:, :, :half].reshape(MAXLEN, half)
    values = kv[:, :, half:].reshape(MAXLEN, half)
    q = q_ref[0]
    scores = lax.dot_general(
        q, keys, (((1,), (1,)), ((), ())), preferred_element_type=jnp.float32
    ) * (1.0 / math.sqrt(HEAD))
    valid = lax.broadcasted_iota(jnp.int32, scores.shape, 1) < lengths[r]
    masked = jnp.where(valid, scores, -1e30)
    top = jnp.max(masked, axis=1, keepdims=True)
    expos = jnp.where(valid, jnp.exp(masked - top), 0.0)
    total = jnp.sum(expos, axis=1, keepdims=True)
    mix = jnp.dot(expos.astype(jnp.bfloat16), values, preferred_element_type=jnp.float32)
    max_ref[0] = jnp.broadcast_to(top, max_ref.shape[1:])
    tot_ref[0] = jnp.broadcast_to(total, tot_ref.shape[1:])
    mix_ref[0] = mix


def paged_attend(query_rows, tables, lengths, pool):
    count = query_rows.shape[0]
    group_size = HEADS // KV_HEADS
    half = KV_HEADS * HEAD
    heads = query_rows.reshape(count, KV_HEADS, group_size, 1, HEAD)
    mask = (jnp.arange(KV_HEADS)[:, None] == jnp.arange(KV_HEADS)[None, :])
    spread = jnp.where(
        mask[None, :, None, :, None], heads, jnp.zeros((), query_rows.dtype)
    ).reshape(count, HEADS, half)
    kv_width = pool.shape[2]
    grid_spec = pltpu.PrefetchScalarGridSpec(
        num_scalar_prefetch=2,
        grid=(count,),
        in_specs=[
            pl.BlockSpec((1, HEADS, half), lambda r, t, l: (r, 0, 0)),
            pl.BlockSpec(memory_space=pl.ANY),
        ],
        out_specs=[
            pl.BlockSpec((1, HEADS, 128), lambda r, t, l: (r, 0, 0)),
            pl.BlockSpec((1, HEADS, 128), lambda r, t, l: (r, 0, 0)),
            pl.BlockSpec((1, HEADS, half), lambda r, t, l: (r, 0, 0)),
        ],
        scratch_shapes=[
            pltpu.VMEM((2, NPAGE, PAGE, kv_width), pool.dtype),
            pltpu.SemaphoreType.DMA((2,)),
        ],
    )
    top, total, mix = pl.pallas_call(
        attend_kernel,
        grid_spec=grid_spec,
        out_shape=[
            jax.ShapeDtypeStruct((count, HEADS, 128), jnp.float32),
            jax.ShapeDtypeStruct((count, HEADS, 128), jnp.float32),
            jax.ShapeDtypeStruct((count, HEADS, half), jnp.float32),
        ],
        compiler_params=pltpu.CompilerParams(dimension_semantics=("arbitrary",)),
        cost_estimate=pl.CostEstimate(
            flops=count * 4 * HEADS * MAXLEN * half,
            transcendentals=count * HEADS * MAXLEN,
            bytes_accessed=count * MAXLEN * kv_width * 2,
        ),
    )(tables, lengths, spread, pool)
    blocks = mix.reshape(count, KV_HEADS, group_size, KV_HEADS, HEAD)
    mixture = jnp.sum(jnp.where(mask[None, :, None, :, None], blocks, 0.0), axis=3)
    return (
        top[:, :, 0].reshape(count, KV_HEADS, group_size),
        total[:, :, 0].reshape(count, KV_HEADS, group_size),
        mixture,
    )


def in_one_piece(arrays, axis, split_dim, concat_dim, along):
    columns = [a.reshape(*a.shape[:along], -1) for a in arrays]
    both = jnp.concatenate(columns, axis=along)
    result, at, gathered = (
        lax.all_to_all(both, axis, split_axis=split_dim, concat_axis=concat_dim, tiled=True),
        0,
        [],
    )
    for a, column in zip(arrays, columns):
        share = result[..., at : at + column.shape[along]]
        gathered.append(share.reshape(*share.shape[:along], *a.shape[along:]))
        at += column.shape[along]
    return tuple(gathered)


def side_by_side(arrays, axis, dim, along):
    widths = [math.prod(a.shape[along:]) for a in arrays]
    both = jnp.concatenate(
        [a.reshape(*a.shape[:along], w) for a, w in zip(arrays, widths)], axis=along
    )
    result = lax.all_gather(both, axis, axis=dim, tiled=True)
    blocks = jnp.split(result, [sum(widths[:k]) for k in range(1, len(widths))], axis=along)
    return tuple(
        (b.reshape(*result.shape[:along], *a.shape[along:]) for a, b in zip(arrays, blocks))
    )


def partial_attend(query_heads, keyval, lengths):
    count_req, positions, kv_width = keyval.shape
    kv_count = query_heads.shape[1]
    head_size = query_heads.shape[3]
    half_width = kv_count * head_size
    key_rows = keyval[:, :, :half_width].reshape(count_req, positions, kv_count, head_size)
    value_rows = keyval[:, :, half_width:].reshape(count_req, positions, kv_count, head_size)
    scores = jnp.einsum(
        "nkgh,ntkh->nkgt", query_heads, key_rows, preferred_element_type=jnp.float32
    ) * (1.0 / math.sqrt(head_size))
    valid = (jnp.arange(positions)[None, :] < lengths[:, None])[:, None, None, :]
    masked = jnp.where(valid, scores, -1e30)
    cache_max = jnp.max(masked, axis=3)
    expos = jnp.where(valid, jnp.exp(masked - cache_max[..., None]), 0.0)
    totals = jnp.sum(expos, axis=3)
    weights = expos.astype(jnp.bfloat16)
    mixture = jnp.einsum("nkgt,ntkh->nkgh", weights, value_rows, preferred_element_type=jnp.float32)
    return (cache_max, totals, mixture)


def finish(query_heads, fresh, cache_max, totals, mixture):
    count_req, kv_count, group_size, head_size = query_heads.shape
    half_width = kv_count * head_size
    own_key = fresh[:, :half_width].reshape(count_req, kv_count, head_size)
    own_value = fresh[:, half_width:].reshape(count_req, kv_count, head_size).astype(jnp.float32)
    own_score = jnp.einsum(
        "nkgh,nkh->nkg", query_heads, own_key, preferred_element_type=jnp.float32
    ) * (1.0 / math.sqrt(head_size))
    highest = jnp.maximum(cache_max, own_score)
    old_share = jnp.exp(cache_max - highest)
    new_share = jnp.exp(own_score - highest)
    weighted = old_share[..., None] * mixture + new_share[..., None] * own_value[:, :, None, :]
    output = weighted / (old_share * totals + new_share)[..., None]
    return output.reshape(count_req, kv_count * group_size * head_size).astype(jnp.bfloat16)


def body(
    queries,
    new_kv,
    cache_pool,
    cache_len,
    local_pages,
    anchor,
    push_pages,
    prefill_attn,
    residual,
    out_weight,
    norm_gain,
    router,
    routes,
    gate_up,
    down_proj,
):
    columns = lax.axis_size("gy")
    slot_count = (MOVED + columns - 2) // (columns - 1)
    group_size = HEADS // KV_HEADS
    kv_width = 2 * KV_HEADS * HEAD
    query_heads = queries.reshape(R_DEV, KV_HEADS, group_size, HEAD)
    matches = (anchor[:, None] == jnp.arange(columns, dtype=jnp.int32)[None, :]).astype(jnp.int32)
    earlier = jnp.sum((jnp.cumsum(matches, axis=0) - 1) * matches, axis=1)
    chosen = anchor * slot_count + earlier
    local_max, local_totals, local_mix = paged_attend(
        queries[:LOCAL], local_pages, cache_len[:LOCAL], cache_pool
    )
    picker = chosen[:, None] == jnp.arange(columns * slot_count, dtype=jnp.int32)[None, :]
    sent_queries = jnp.einsum(
        "ms,md->sd",
        picker.astype(jnp.bfloat16),
        queries[LOCAL:],
        preferred_element_type=jnp.float32,
    )
    sent_lengths = jnp.sum(
        jnp.where(picker, cache_len[LOCAL:, None].astype(jnp.float32), 0.0), axis=0
    )
    got_queries, got_lengths = in_one_piece(
        (sent_queries.reshape(columns, slot_count, D), sent_lengths.reshape(columns, slot_count)),
        "gy",
        0,
        0,
        2,
    )
    far_max, far_totals, far_mix = paged_attend(
        got_queries.astype(jnp.bfloat16).reshape(columns * slot_count, D),
        push_pages,
        got_lengths.reshape(columns * slot_count).astype(jnp.int32),
        cache_pool,
    )
    back_max, back_totals, back_mix = in_one_piece(
        (
            far_max.reshape(columns, slot_count, KV_HEADS, group_size),
            far_totals.reshape(columns, slot_count, KV_HEADS, group_size),
            far_mix.reshape(columns, slot_count, KV_HEADS, group_size, HEAD),
        ),
        "gy",
        0,
        0,
        4,
    )
    cache_max = jnp.concatenate(
        [local_max, back_max.reshape(columns * slot_count, KV_HEADS, group_size)[chosen]], axis=0
    )
    totals = jnp.concatenate(
        [local_totals, back_totals.reshape(columns * slot_count, KV_HEADS, group_size)[chosen]],
        axis=0,
    )
    mixture = jnp.concatenate(
        [local_mix, back_mix.reshape(columns * slot_count, KV_HEADS, group_size, HEAD)[chosen]],
        axis=0,
    )
    attended = finish(query_heads, new_kv, cache_max, totals, mixture)
    tokens = jnp.concatenate([attended, prefill_attn], axis=0)
    row_count = tokens.shape[0]
    full_out = lax.all_gather(out_weight, "gx", axis=0, tiled=True)
    full_pair = lax.all_gather(gate_up, "gx", axis=0, tiled=True)
    full_down = lax.all_gather(down_proj, "gx", axis=0, tiled=True)
    stream = residual.astype(jnp.float32) + jnp.dot(
        tokens, full_out, preferred_element_type=jnp.float32
    )
    normed = (
        stream
        * lax.rsqrt(jnp.mean(stream * stream, axis=1, keepdims=True) + 1e-06)
        * norm_gain.astype(jnp.float32)
    ).astype(jnp.bfloat16)
    logits = jnp.dot(normed, router, preferred_element_type=jnp.float32)
    selector = routes[:, :, None] == jnp.arange(EXPERTS, dtype=jnp.int32)[None, None, :]
    gate_weights = jax.nn.softmax(
        jnp.sum(jnp.where(selector, logits[:, None, :], 0.0), axis=2), axis=1
    )
    row_hits = jnp.any(selector, axis=1)
    earlier_rows = (
        lax.broadcasted_iota(jnp.int32, (row_count, row_count), 1)
        < lax.broadcasted_iota(jnp.int32, (row_count, row_count), 0)
    ).astype(jnp.bfloat16)
    counts = jnp.dot(
        earlier_rows, row_hits.astype(jnp.bfloat16), preferred_element_type=jnp.float32
    ).astype(jnp.int32)
    place_of = jnp.sum(jnp.where(selector, counts[:, None, :], 0), axis=2)
    targets = (routes * CAP + place_of).reshape(row_count * TOP)
    experts_dev = full_pair.shape[1]
    slot_hits = row_hits.T[:, None, :] & (
        counts.T[:, None, :] == jnp.arange(CAP, dtype=jnp.int32)[None, :, None]
    )
    outgoing_rows = (
        jnp.einsum(
            "ecr,rd->ecd",
            slot_hits.astype(jnp.bfloat16),
            normed,
            preferred_element_type=jnp.float32,
        )
        .astype(jnp.bfloat16)
        .reshape(columns, experts_dev, CAP, D)
    )
    arrived = lax.all_to_all(outgoing_rows, "gy", split_axis=0, concat_axis=0, tiled=True)
    gate_pair = jnp.einsum("secd,def->secf", arrived, full_pair, preferred_element_type=jnp.float32)
    hidden = (jax.nn.silu(gate_pair[..., :FF]) * gate_pair[..., FF:]).astype(jnp.bfloat16)
    expert_rows = jnp.einsum(
        "secf,def->secd", hidden, full_down, preferred_element_type=jnp.float32
    ).astype(jnp.bfloat16)
    returned = lax.all_to_all(expert_rows, "gy", split_axis=0, concat_axis=0, tiled=True).reshape(
        EXPERTS * CAP, D
    )
    picked = returned[targets].astype(jnp.float32).reshape(row_count, TOP, D)
    layer_out = stream + jnp.sum(gate_weights[:, :, None] * picked, axis=1)
    return (attended, layer_out)


def solution(mesh):
    placed = (
        P(("gx", "gy"), None),
        P(("gx", "gy"), None),
        P(("gx", "gy"), None, None),
        P(("gx", "gy")),
        P(("gx", "gy"), None),
        P(("gx", "gy")),
        P(("gx", "gy"), None),
        P(("gx", "gy"), None),
        P(("gx", "gy"), None),
        P("gx", None),
        P(),
        P(),
        P(("gx", "gy"), None),
        P("gx", "gy", None),
        P("gx", "gy", None),
    )
    return jax.shard_map(
        body,
        mesh=mesh,
        in_specs=placed,
        out_specs=(P(("gx", "gy"), None), P(("gx", "gy"), None)),
        check_vma=False,
    )
```

```python
import math

import jax
import jax.numpy as jnp
from jax import lax
from jax.sharding import PartitionSpec as P
from jax.experimental import pallas as pl
from jax.experimental.pallas import tpu as pltpu

D = 1536
HEADS = 24
KV_HEADS = 8
HEAD = 64
EXPERTS = 32
FF = 512
TOP = 8
MAXLEN = 512
R_DEV = 16
LOCAL = 8
MOVED = 8
CAP = 48
NPAGE = 32
PAGE = 16


def attend_kernel(tables, lengths, q_ref, pool_ref, max_ref, tot_ref, mix_ref, kvbuf, sems):
    r = pl.program_id(0)
    n = pl.num_programs(0)
    half = KV_HEADS * HEAD

    def start(req, slot):
        def one(p, carry):
            pltpu.make_async_copy(
                pool_ref.at[tables[req, p]], kvbuf.at[slot, p], sems.at[slot]
            ).start()
            return carry

        lax.fori_loop(0, NPAGE, one, 0, unroll=8)

    @pl.when(r == 0)
    def _():
        start(0, 0)

    slot = r % 2

    @pl.when(r + 1 < n)
    def _():
        start(r + 1, 1 - slot)

    pltpu.make_async_copy(pool_ref.at[pl.ds(0, NPAGE)], kvbuf.at[slot], sems.at[slot]).wait()
    kv = kvbuf.at[slot]
    keys = kv[:, :, :half].reshape(MAXLEN, half)
    values = kv[:, :, half:].reshape(MAXLEN, half)
    q = q_ref[0]
    scores = lax.dot_general(
        q, keys, (((1,), (1,)), ((), ())), preferred_element_type=jnp.float32
    ) * (1.0 / math.sqrt(HEAD))
    valid = lax.broadcasted_iota(jnp.int32, scores.shape, 1) < lengths[r]
    masked = jnp.where(valid, scores, -1e30)
    top = jnp.max(masked, axis=1, keepdims=True)
    expos = jnp.where(valid, jnp.exp(masked - top), 0.0)
    total = jnp.sum(expos, axis=1, keepdims=True)
    mix = jnp.dot(expos.astype(jnp.bfloat16), values, preferred_element_type=jnp.float32)
    max_ref[0] = jnp.broadcast_to(top, max_ref.shape[1:])
    tot_ref[0] = jnp.broadcast_to(total, tot_ref.shape[1:])
    mix_ref[0] = mix


def exchange_kernel(x_ref, y_ref, send_sems, recv_sems, own_sem):
    n = x_ref.shape[0]
    me = lax.axis_index("gy")
    row = lax.axis_index("gx")
    mesh_ids = pl.DeviceIdType.MESH
    barrier = pltpu.get_barrier_semaphore()
    for k in range(1, n):
        pl.semaphore_signal(
            barrier, inc=1, device_id=(row, lax.rem(me + k, n)), device_id_type=mesh_ids
        )
    pl.semaphore_wait(barrier, n - 1)
    own = pltpu.make_async_copy(x_ref.at[me], y_ref.at[me], own_sem)
    own.start()
    copies = []
    for k in range(1, n):
        dest = lax.rem(me + k, n)
        copy = pltpu.make_async_remote_copy(
            src_ref=x_ref.at[dest],
            dst_ref=y_ref.at[me],
            send_sem=send_sems.at[k],
            recv_sem=recv_sems.at[k],
            device_id=(row, dest),
            device_id_type=mesh_ids,
        )
        copy.start()
        copies.append(copy)
    for k in range(1, n):
        source = lax.rem(me + n - k, n)
        pltpu.make_async_remote_copy(
            src_ref=x_ref.at[source],
            dst_ref=y_ref.at[source],
            send_sem=send_sems.at[k],
            recv_sem=recv_sems.at[k],
            device_id=(row, source),
            device_id_type=mesh_ids,
        ).wait_recv()
    for copy in copies:
        copy.wait_send()
    own.wait()


def exchange(x, tag):
    n = x.shape[0]
    block = x.size // n * x.dtype.itemsize
    return pl.pallas_call(
        exchange_kernel,
        out_shape=jax.ShapeDtypeStruct(x.shape, x.dtype),
        in_specs=[pl.BlockSpec(memory_space=pl.ANY)],
        out_specs=pl.BlockSpec(memory_space=pl.ANY),
        scratch_shapes=[
            pltpu.SemaphoreType.DMA((n,)),
            pltpu.SemaphoreType.DMA((n,)),
            pltpu.SemaphoreType.DMA,
        ],
        compiler_params=pltpu.CompilerParams(collective_id=tag, has_side_effects=True),
        cost_estimate=pl.CostEstimate(
            flops=0, transcendentals=0, bytes_accessed=2 * n * block
        ),
    )(x)


def paged_attend(query_rows, tables, lengths, pool):
    count = query_rows.shape[0]
    group_size = HEADS // KV_HEADS
    half = KV_HEADS * HEAD
    heads = query_rows.reshape(count, KV_HEADS, group_size, 1, HEAD)
    mask = (jnp.arange(KV_HEADS)[:, None] == jnp.arange(KV_HEADS)[None, :])
    spread = jnp.where(
        mask[None, :, None, :, None], heads, jnp.zeros((), query_rows.dtype)
    ).reshape(count, HEADS, half)
    kv_width = pool.shape[2]
    grid_spec = pltpu.PrefetchScalarGridSpec(
        num_scalar_prefetch=2,
        grid=(count,),
        in_specs=[
            pl.BlockSpec((1, HEADS, half), lambda r, t, l: (r, 0, 0)),
            pl.BlockSpec(memory_space=pl.ANY),
        ],
        out_specs=[
            pl.BlockSpec((1, HEADS, 128), lambda r, t, l: (r, 0, 0)),
            pl.BlockSpec((1, HEADS, 128), lambda r, t, l: (r, 0, 0)),
            pl.BlockSpec((1, HEADS, half), lambda r, t, l: (r, 0, 0)),
        ],
        scratch_shapes=[
            pltpu.VMEM((2, NPAGE, PAGE, kv_width), pool.dtype),
            pltpu.SemaphoreType.DMA((2,)),
        ],
    )
    top, total, mix = pl.pallas_call(
        attend_kernel,
        grid_spec=grid_spec,
        out_shape=[
            jax.ShapeDtypeStruct((count, HEADS, 128), jnp.float32),
            jax.ShapeDtypeStruct((count, HEADS, 128), jnp.float32),
            jax.ShapeDtypeStruct((count, HEADS, half), jnp.float32),
        ],
        compiler_params=pltpu.CompilerParams(dimension_semantics=("arbitrary",)),
        cost_estimate=pl.CostEstimate(
            flops=count * 4 * HEADS * MAXLEN * half,
            transcendentals=count * HEADS * MAXLEN,
            bytes_accessed=count * MAXLEN * kv_width * 2,
        ),
    )(tables, lengths, spread, pool)
    blocks = mix.reshape(count, KV_HEADS, group_size, KV_HEADS, HEAD)
    mixture = jnp.sum(jnp.where(mask[None, :, None, :, None], blocks, 0.0), axis=3)
    return (
        top[:, :, 0].reshape(count, KV_HEADS, group_size),
        total[:, :, 0].reshape(count, KV_HEADS, group_size),
        mixture,
    )


def in_one_piece(arrays, axis, split_dim, concat_dim, along):
    columns = [a.reshape(*a.shape[:along], -1) for a in arrays]
    both = jnp.concatenate(columns, axis=along)
    result, at, gathered = (
        lax.all_to_all(both, axis, split_axis=split_dim, concat_axis=concat_dim, tiled=True),
        0,
        [],
    )
    for a, column in zip(arrays, columns):
        share = result[..., at : at + column.shape[along]]
        gathered.append(share.reshape(*share.shape[:along], *a.shape[along:]))
        at += column.shape[along]
    return tuple(gathered)


def side_by_side(arrays, axis, dim, along):
    widths = [math.prod(a.shape[along:]) for a in arrays]
    both = jnp.concatenate(
        [a.reshape(*a.shape[:along], w) for a, w in zip(arrays, widths)], axis=along
    )
    result = lax.all_gather(both, axis, axis=dim, tiled=True)
    blocks = jnp.split(result, [sum(widths[:k]) for k in range(1, len(widths))], axis=along)
    return tuple(
        (b.reshape(*result.shape[:along], *a.shape[along:]) for a, b in zip(arrays, blocks))
    )


def partial_attend(query_heads, keyval, lengths):
    count_req, positions, kv_width = keyval.shape
    kv_count = query_heads.shape[1]
    head_size = query_heads.shape[3]
    half_width = kv_count * head_size
    key_rows = keyval[:, :, :half_width].reshape(count_req, positions, kv_count, head_size)
    value_rows = keyval[:, :, half_width:].reshape(count_req, positions, kv_count, head_size)
    scores = jnp.einsum(
        "nkgh,ntkh->nkgt", query_heads, key_rows, preferred_element_type=jnp.float32
    ) * (1.0 / math.sqrt(head_size))
    valid = (jnp.arange(positions)[None, :] < lengths[:, None])[:, None, None, :]
    masked = jnp.where(valid, scores, -1e30)
    cache_max = jnp.max(masked, axis=3)
    expos = jnp.where(valid, jnp.exp(masked - cache_max[..., None]), 0.0)
    totals = jnp.sum(expos, axis=3)
    weights = expos.astype(jnp.bfloat16)
    mixture = jnp.einsum("nkgt,ntkh->nkgh", weights, value_rows, preferred_element_type=jnp.float32)
    return (cache_max, totals, mixture)


def finish(query_heads, fresh, cache_max, totals, mixture):
    count_req, kv_count, group_size, head_size = query_heads.shape
    half_width = kv_count * head_size
    own_key = fresh[:, :half_width].reshape(count_req, kv_count, head_size)
    own_value = fresh[:, half_width:].reshape(count_req, kv_count, head_size).astype(jnp.float32)
    own_score = jnp.einsum(
        "nkgh,nkh->nkg", query_heads, own_key, preferred_element_type=jnp.float32
    ) * (1.0 / math.sqrt(head_size))
    highest = jnp.maximum(cache_max, own_score)
    old_share = jnp.exp(cache_max - highest)
    new_share = jnp.exp(own_score - highest)
    weighted = old_share[..., None] * mixture + new_share[..., None] * own_value[:, :, None, :]
    output = weighted / (old_share * totals + new_share)[..., None]
    return output.reshape(count_req, kv_count * group_size * head_size).astype(jnp.bfloat16)


def body(
    queries,
    new_kv,
    cache_pool,
    cache_len,
    local_pages,
    anchor,
    push_pages,
    prefill_attn,
    residual,
    out_weight,
    norm_gain,
    router,
    routes,
    gate_up,
    down_proj,
):
    columns = lax.axis_size("gy")
    slot_count = (MOVED + columns - 2) // (columns - 1)
    group_size = HEADS // KV_HEADS
    kv_width = 2 * KV_HEADS * HEAD
    query_heads = queries.reshape(R_DEV, KV_HEADS, group_size, HEAD)
    matches = (anchor[:, None] == jnp.arange(columns, dtype=jnp.int32)[None, :]).astype(jnp.int32)
    earlier = jnp.sum((jnp.cumsum(matches, axis=0) - 1) * matches, axis=1)
    chosen = anchor * slot_count + earlier
    local_max, local_totals, local_mix = paged_attend(
        queries[:LOCAL], local_pages, cache_len[:LOCAL], cache_pool
    )
    picker = chosen[:, None] == jnp.arange(columns * slot_count, dtype=jnp.int32)[None, :]
    sent_queries = jnp.einsum(
        "ms,md->sd",
        picker.astype(jnp.bfloat16),
        queries[LOCAL:],
        preferred_element_type=jnp.float32,
    )
    sent_lengths = jnp.sum(
        jnp.where(picker, cache_len[LOCAL:, None].astype(jnp.float32), 0.0), axis=0
    )
    got_queries, got_lengths = in_one_piece(
        (sent_queries.reshape(columns, slot_count, D), sent_lengths.reshape(columns, slot_count)),
        "gy",
        0,
        0,
        2,
    )
    far_max, far_totals, far_mix = paged_attend(
        got_queries.astype(jnp.bfloat16).reshape(columns * slot_count, D),
        push_pages,
        got_lengths.reshape(columns * slot_count).astype(jnp.int32),
        cache_pool,
    )
    back_max, back_totals, back_mix = in_one_piece(
        (
            far_max.reshape(columns, slot_count, KV_HEADS, group_size),
            far_totals.reshape(columns, slot_count, KV_HEADS, group_size),
            far_mix.reshape(columns, slot_count, KV_HEADS, group_size, HEAD),
        ),
        "gy",
        0,
        0,
        4,
    )
    cache_max = jnp.concatenate(
        [local_max, back_max.reshape(columns * slot_count, KV_HEADS, group_size)[chosen]], axis=0
    )
    totals = jnp.concatenate(
        [local_totals, back_totals.reshape(columns * slot_count, KV_HEADS, group_size)[chosen]],
        axis=0,
    )
    mixture = jnp.concatenate(
        [local_mix, back_mix.reshape(columns * slot_count, KV_HEADS, group_size, HEAD)[chosen]],
        axis=0,
    )
    attended = finish(query_heads, new_kv, cache_max, totals, mixture)
    tokens = jnp.concatenate([attended, prefill_attn], axis=0)
    row_count = tokens.shape[0]
    full_out = lax.all_gather(out_weight, "gx", axis=0, tiled=True)
    full_pair = lax.all_gather(gate_up, "gx", axis=0, tiled=True)
    full_down = lax.all_gather(down_proj, "gx", axis=0, tiled=True)
    stream = residual.astype(jnp.float32) + jnp.dot(
        tokens, full_out, preferred_element_type=jnp.float32
    )
    normed = (
        stream
        * lax.rsqrt(jnp.mean(stream * stream, axis=1, keepdims=True) + 1e-06)
        * norm_gain.astype(jnp.float32)
    ).astype(jnp.bfloat16)
    logits = jnp.dot(normed, router, preferred_element_type=jnp.float32)
    selector = routes[:, :, None] == jnp.arange(EXPERTS, dtype=jnp.int32)[None, None, :]
    gate_weights = jax.nn.softmax(
        jnp.sum(jnp.where(selector, logits[:, None, :], 0.0), axis=2), axis=1
    )
    row_hits = jnp.any(selector, axis=1)
    earlier_rows = (
        lax.broadcasted_iota(jnp.int32, (row_count, row_count), 1)
        < lax.broadcasted_iota(jnp.int32, (row_count, row_count), 0)
    ).astype(jnp.bfloat16)
    counts = jnp.dot(
        earlier_rows, row_hits.astype(jnp.bfloat16), preferred_element_type=jnp.float32
    ).astype(jnp.int32)
    place_of = jnp.sum(jnp.where(selector, counts[:, None, :], 0), axis=2)
    targets = (routes * CAP + place_of).reshape(row_count * TOP)
    experts_dev = full_pair.shape[1]
    slot_hits = row_hits.T[:, None, :] & (
        counts.T[:, None, :] == jnp.arange(CAP, dtype=jnp.int32)[None, :, None]
    )
    outgoing_rows = (
        jnp.einsum(
            "ecr,rd->ecd",
            slot_hits.astype(jnp.bfloat16),
            normed,
            preferred_element_type=jnp.float32,
        )
        .astype(jnp.bfloat16)
        .reshape(columns, experts_dev, CAP, D)
    )
    arrived = exchange(outgoing_rows, 1)
    gate_pair = jnp.einsum("secd,def->secf", arrived, full_pair, preferred_element_type=jnp.float32)
    hidden = (jax.nn.silu(gate_pair[..., :FF]) * gate_pair[..., FF:]).astype(jnp.bfloat16)
    expert_rows = jnp.einsum(
        "secf,def->secd", hidden, full_down, preferred_element_type=jnp.float32
    ).astype(jnp.bfloat16)
    returned = exchange(expert_rows, 2).reshape(
        EXPERTS * CAP, D
    )
    picked = returned[targets].astype(jnp.float32).reshape(row_count, TOP, D)
    layer_out = stream + jnp.sum(gate_weights[:, :, None] * picked, axis=1)
    return (attended, layer_out)


def solution(mesh):
    placed = (
        P(("gx", "gy"), None),
        P(("gx", "gy"), None),
        P(("gx", "gy"), None, None),
        P(("gx", "gy")),
        P(("gx", "gy"), None),
        P(("gx", "gy")),
        P(("gx", "gy"), None),
        P(("gx", "gy"), None),
        P(("gx", "gy"), None),
        P("gx", None),
        P(),
        P(),
        P(("gx", "gy"), None),
        P("gx", "gy", None),
        P("gx", "gy", None),
    )
    return jax.shard_map(
        body,
        mesh=mesh,
        in_specs=placed,
        out_specs=(P(("gx", "gy"), None), P(("gx", "gy"), None)),
        check_vma=False,
    )
```

```python
import math

import jax
import jax.numpy as jnp
from jax import lax
from jax.sharding import PartitionSpec as P
from jax.experimental import pallas as pl
from jax.experimental.pallas import tpu as pltpu

D = 1536
HEADS = 24
KV_HEADS = 8
HEAD = 64
EXPERTS = 32
FF = 512
TOP = 8
MAXLEN = 512
R_DEV = 16
LOCAL = 8
MOVED = 8
CAP = 48
NPAGE = 32
PAGE = 16


def attend_kernel(tables, lengths, q_ref, pool_ref, max_ref, tot_ref, mix_ref, kvbuf, sems):
    r = pl.program_id(0)
    n = pl.num_programs(0)
    half = KV_HEADS * HEAD

    def start(req, slot):
        def one(p, carry):
            pltpu.make_async_copy(
                pool_ref.at[tables[req, p]], kvbuf.at[slot, p], sems.at[slot]
            ).start()
            return carry

        lax.fori_loop(0, NPAGE, one, 0, unroll=8)

    @pl.when(r == 0)
    def _():
        start(0, 0)

    slot = r % 2

    @pl.when(r + 1 < n)
    def _():
        start(r + 1, 1 - slot)

    pltpu.make_async_copy(pool_ref.at[pl.ds(0, NPAGE)], kvbuf.at[slot], sems.at[slot]).wait()
    kv = kvbuf.at[slot]
    keys = kv[:, :, :half].reshape(MAXLEN, half)
    values = kv[:, :, half:].reshape(MAXLEN, half)
    q = q_ref[0]
    scores = lax.dot_general(
        q, keys, (((1,), (1,)), ((), ())), preferred_element_type=jnp.float32
    ) * (1.0 / math.sqrt(HEAD))
    valid = lax.broadcasted_iota(jnp.int32, scores.shape, 1) < lengths[r]
    masked = jnp.where(valid, scores, -1e30)
    top = jnp.max(masked, axis=1, keepdims=True)
    expos = jnp.where(valid, jnp.exp(masked - top), 0.0)
    total = jnp.sum(expos, axis=1, keepdims=True)
    mix = jnp.dot(expos.astype(jnp.bfloat16), values, preferred_element_type=jnp.float32)
    max_ref[0] = jnp.broadcast_to(top, max_ref.shape[1:])
    tot_ref[0] = jnp.broadcast_to(total, tot_ref.shape[1:])
    mix_ref[0] = mix


def paged_attend(query_rows, tables, lengths, pool):
    count = query_rows.shape[0]
    group_size = HEADS // KV_HEADS
    half = KV_HEADS * HEAD
    heads = query_rows.reshape(count, KV_HEADS, group_size, 1, HEAD)
    mask = (jnp.arange(KV_HEADS)[:, None] == jnp.arange(KV_HEADS)[None, :])
    spread = jnp.where(
        mask[None, :, None, :, None], heads, jnp.zeros((), query_rows.dtype)
    ).reshape(count, HEADS, half)
    kv_width = pool.shape[2]
    grid_spec = pltpu.PrefetchScalarGridSpec(
        num_scalar_prefetch=2,
        grid=(count,),
        in_specs=[
            pl.BlockSpec((1, HEADS, half), lambda r, t, l: (r, 0, 0)),
            pl.BlockSpec(memory_space=pl.ANY),
        ],
        out_specs=[
            pl.BlockSpec((1, HEADS, 128), lambda r, t, l: (r, 0, 0)),
            pl.BlockSpec((1, HEADS, 128), lambda r, t, l: (r, 0, 0)),
            pl.BlockSpec((1, HEADS, half), lambda r, t, l: (r, 0, 0)),
        ],
        scratch_shapes=[
            pltpu.VMEM((2, NPAGE, PAGE, kv_width), pool.dtype),
            pltpu.SemaphoreType.DMA((2,)),
        ],
    )
    top, total, mix = pl.pallas_call(
        attend_kernel,
        grid_spec=grid_spec,
        out_shape=[
            jax.ShapeDtypeStruct((count, HEADS, 128), jnp.float32),
            jax.ShapeDtypeStruct((count, HEADS, 128), jnp.float32),
            jax.ShapeDtypeStruct((count, HEADS, half), jnp.float32),
        ],
        compiler_params=pltpu.CompilerParams(dimension_semantics=("arbitrary",)),
        cost_estimate=pl.CostEstimate(
            flops=count * 4 * HEADS * MAXLEN * half,
            transcendentals=count * HEADS * MAXLEN,
            bytes_accessed=count * MAXLEN * kv_width * 2,
        ),
    )(tables, lengths, spread, pool)
    blocks = mix.reshape(count, KV_HEADS, group_size, KV_HEADS, HEAD)
    mixture = jnp.sum(jnp.where(mask[None, :, None, :, None], blocks, 0.0), axis=3)
    return (
        top[:, :, 0].reshape(count, KV_HEADS, group_size),
        total[:, :, 0].reshape(count, KV_HEADS, group_size),
        mixture,
    )


def in_one_piece(arrays, axis, split_dim, concat_dim, along):
    columns = [a.reshape(*a.shape[:along], -1) for a in arrays]
    both = jnp.concatenate(columns, axis=along)
    result, at, gathered = (
        lax.all_to_all(both, axis, split_axis=split_dim, concat_axis=concat_dim, tiled=True),
        0,
        [],
    )
    for a, column in zip(arrays, columns):
        share = result[..., at : at + column.shape[along]]
        gathered.append(share.reshape(*share.shape[:along], *a.shape[along:]))
        at += column.shape[along]
    return tuple(gathered)


def side_by_side(arrays, axis, dim, along):
    widths = [math.prod(a.shape[along:]) for a in arrays]
    both = jnp.concatenate(
        [a.reshape(*a.shape[:along], w) for a, w in zip(arrays, widths)], axis=along
    )
    result = lax.all_gather(both, axis, axis=dim, tiled=True)
    blocks = jnp.split(result, [sum(widths[:k]) for k in range(1, len(widths))], axis=along)
    return tuple(
        (b.reshape(*result.shape[:along], *a.shape[along:]) for a, b in zip(arrays, blocks))
    )


def partial_attend(query_heads, keyval, lengths):
    count_req, positions, kv_width = keyval.shape
    kv_count = query_heads.shape[1]
    head_size = query_heads.shape[3]
    half_width = kv_count * head_size
    key_rows = keyval[:, :, :half_width].reshape(count_req, positions, kv_count, head_size)
    value_rows = keyval[:, :, half_width:].reshape(count_req, positions, kv_count, head_size)
    scores = jnp.einsum(
        "nkgh,ntkh->nkgt", query_heads, key_rows, preferred_element_type=jnp.float32
    ) * (1.0 / math.sqrt(head_size))
    valid = (jnp.arange(positions)[None, :] < lengths[:, None])[:, None, None, :]
    masked = jnp.where(valid, scores, -1e30)
    cache_max = jnp.max(masked, axis=3)
    expos = jnp.where(valid, jnp.exp(masked - cache_max[..., None]), 0.0)
    totals = jnp.sum(expos, axis=3)
    weights = expos.astype(jnp.bfloat16)
    mixture = jnp.einsum("nkgt,ntkh->nkgh", weights, value_rows, preferred_element_type=jnp.float32)
    return (cache_max, totals, mixture)


def finish(query_heads, fresh, cache_max, totals, mixture):
    count_req, kv_count, group_size, head_size = query_heads.shape
    half_width = kv_count * head_size
    own_key = fresh[:, :half_width].reshape(count_req, kv_count, head_size)
    own_value = fresh[:, half_width:].reshape(count_req, kv_count, head_size).astype(jnp.float32)
    own_score = jnp.einsum(
        "nkgh,nkh->nkg", query_heads, own_key, preferred_element_type=jnp.float32
    ) * (1.0 / math.sqrt(head_size))
    highest = jnp.maximum(cache_max, own_score)
    old_share = jnp.exp(cache_max - highest)
    new_share = jnp.exp(own_score - highest)
    weighted = old_share[..., None] * mixture + new_share[..., None] * own_value[:, :, None, :]
    output = weighted / (old_share * totals + new_share)[..., None]
    return output.reshape(count_req, kv_count * group_size * head_size).astype(jnp.bfloat16)


def body(
    queries,
    new_kv,
    cache_pool,
    cache_len,
    local_pages,
    anchor,
    push_pages,
    prefill_attn,
    residual,
    out_weight,
    norm_gain,
    router,
    routes,
    gate_up,
    down_proj,
):
    columns = lax.axis_size("gy")
    slot_count = (MOVED + columns - 2) // (columns - 1)
    group_size = HEADS // KV_HEADS
    kv_width = 2 * KV_HEADS * HEAD
    query_heads = queries.reshape(R_DEV, KV_HEADS, group_size, HEAD)
    matches = (anchor[:, None] == jnp.arange(columns, dtype=jnp.int32)[None, :]).astype(jnp.int32)
    earlier = jnp.sum((jnp.cumsum(matches, axis=0) - 1) * matches, axis=1)
    chosen = anchor * slot_count + earlier
    local_max, local_totals, local_mix = paged_attend(
        queries[:LOCAL], local_pages, cache_len[:LOCAL], cache_pool
    )
    picker = chosen[:, None] == jnp.arange(columns * slot_count, dtype=jnp.int32)[None, :]
    sent_queries = jnp.einsum(
        "ms,md->sd",
        picker.astype(jnp.bfloat16),
        queries[LOCAL:],
        preferred_element_type=jnp.float32,
    )
    sent_lengths = jnp.sum(
        jnp.where(picker, cache_len[LOCAL:, None].astype(jnp.float32), 0.0), axis=0
    )
    got_queries, got_lengths = in_one_piece(
        (sent_queries.reshape(columns, slot_count, D), sent_lengths.reshape(columns, slot_count)),
        "gy",
        0,
        0,
        2,
    )
    far_max, far_totals, far_mix = paged_attend(
        got_queries.astype(jnp.bfloat16).reshape(columns * slot_count, D),
        push_pages,
        got_lengths.reshape(columns * slot_count).astype(jnp.int32),
        cache_pool,
    )
    back_max, back_totals, back_mix = in_one_piece(
        (
            far_max.reshape(columns, slot_count, KV_HEADS, group_size),
            far_totals.reshape(columns, slot_count, KV_HEADS, group_size),
            far_mix.reshape(columns, slot_count, KV_HEADS, group_size, HEAD),
        ),
        "gy",
        0,
        0,
        4,
    )
    cache_max = jnp.concatenate(
        [local_max, back_max.reshape(columns * slot_count, KV_HEADS, group_size)[chosen]], axis=0
    )
    totals = jnp.concatenate(
        [local_totals, back_totals.reshape(columns * slot_count, KV_HEADS, group_size)[chosen]],
        axis=0,
    )
    mixture = jnp.concatenate(
        [local_mix, back_mix.reshape(columns * slot_count, KV_HEADS, group_size, HEAD)[chosen]],
        axis=0,
    )
    attended = finish(query_heads, new_kv, cache_max, totals, mixture)
    tokens = jnp.concatenate([attended, prefill_attn], axis=0)
    row_count = tokens.shape[0]
    full_out = lax.all_gather(out_weight, "gx", axis=0, tiled=True)
    full_pair = lax.all_gather(gate_up, "gx", axis=0, tiled=True)
    full_down = lax.all_gather(down_proj, "gx", axis=0, tiled=True)
    stream = residual.astype(jnp.float32) + jnp.dot(
        tokens, full_out, preferred_element_type=jnp.float32
    )
    normed = (
        stream
        * lax.rsqrt(jnp.mean(stream * stream, axis=1, keepdims=True) + 1e-06)
        * norm_gain.astype(jnp.float32)
    ).astype(jnp.bfloat16)
    logits = jnp.dot(normed, router, preferred_element_type=jnp.float32)
    selector = routes[:, :, None] == jnp.arange(EXPERTS, dtype=jnp.int32)[None, None, :]
    gate_weights = jax.nn.softmax(
        jnp.sum(jnp.where(selector, logits[:, None, :], 0.0), axis=2), axis=1
    )
    row_hits = jnp.any(selector, axis=1)
    earlier_rows = (
        lax.broadcasted_iota(jnp.int32, (row_count, row_count), 1)
        < lax.broadcasted_iota(jnp.int32, (row_count, row_count), 0)
    ).astype(jnp.bfloat16)
    counts = jnp.dot(
        earlier_rows, row_hits.astype(jnp.bfloat16), preferred_element_type=jnp.float32
    ).astype(jnp.int32)
    place_of = jnp.sum(jnp.where(selector, counts[:, None, :], 0), axis=2)
    targets = (routes * CAP + place_of).reshape(row_count * TOP)
    experts_dev = full_pair.shape[1]
    slot_hits = row_hits.T[:, None, :] & (
        counts.T[:, None, :] == jnp.arange(CAP, dtype=jnp.int32)[None, :, None]
    )
    chunk_hits = slot_hits.reshape(columns, experts_dev, CAP, row_count)
    returned_parts = []
    for local in range(experts_dev):
        outgoing = jnp.einsum(
            "scr,rd->scd",
            chunk_hits[:, local].astype(jnp.bfloat16),
            normed,
            preferred_element_type=jnp.float32,
        ).astype(jnp.bfloat16)
        arrived = lax.all_to_all(outgoing, "gy", split_axis=0, concat_axis=0, tiled=True)
        gate_pair = jnp.einsum(
            "scd,df->scf", arrived, full_pair[:, local], preferred_element_type=jnp.float32
        )
        hidden = (jax.nn.silu(gate_pair[..., :FF]) * gate_pair[..., FF:]).astype(jnp.bfloat16)
        expert_rows = jnp.einsum(
            "scf,df->scd", hidden, full_down[:, local], preferred_element_type=jnp.float32
        ).astype(jnp.bfloat16)
        returned_parts.append(
            lax.all_to_all(expert_rows, "gy", split_axis=0, concat_axis=0, tiled=True)
        )
    returned = jnp.stack(returned_parts, axis=1).reshape(EXPERTS * CAP, D)
    picked = returned[targets].astype(jnp.float32).reshape(row_count, TOP, D)
    layer_out = stream + jnp.sum(gate_weights[:, :, None] * picked, axis=1)
    return (attended, layer_out)


def solution(mesh):
    placed = (
        P(("gx", "gy"), None),
        P(("gx", "gy"), None),
        P(("gx", "gy"), None, None),
        P(("gx", "gy")),
        P(("gx", "gy"), None),
        P(("gx", "gy")),
        P(("gx", "gy"), None),
        P(("gx", "gy"), None),
        P(("gx", "gy"), None),
        P("gx", None),
        P(),
        P(),
        P(("gx", "gy"), None),
        P("gx", "gy", None),
        P("gx", "gy", None),
    )
    return jax.shard_map(
        body,
        mesh=mesh,
        in_specs=placed,
        out_specs=(P(("gx", "gy"), None), P(("gx", "gy"), None)),
        check_vma=False,
    )
```

```python
import math

import jax
import jax.numpy as jnp
from jax import lax
from jax.sharding import PartitionSpec as P
from jax.experimental import pallas as pl
from jax.experimental.pallas import tpu as pltpu

D = 1536
HEADS = 24
KV_HEADS = 8
HEAD = 64
EXPERTS = 32
FF = 512
TOP = 8
MAXLEN = 512
R_DEV = 16
LOCAL = 8
MOVED = 8
CAP = 48
NPAGE = 32
PAGE = 16


def attend_kernel(tables, lengths, q_ref, pool_ref, max_ref, tot_ref, mix_ref, kvbuf, sems):
    r = pl.program_id(0)
    n = pl.num_programs(0)
    half = KV_HEADS * HEAD

    def pages_of(req):
        return (lengths[req] + PAGE - 1) // PAGE

    def page_copy(req, slot, p):
        return pltpu.make_async_copy(
            pool_ref.at[tables[req, p]], kvbuf.at[slot, p], sems.at[slot, p]
        )

    def start(req, slot):
        def one(p, carry):
            page_copy(req, slot, p).start()
            return carry

        lax.fori_loop(0, pages_of(req), one, 0)

    @pl.when(r == 0)
    def _():
        kvbuf[...] = jnp.zeros(kvbuf.shape, kvbuf.dtype)
        start(0, 0)

    slot = r % 2

    @pl.when(r + 1 < n)
    def _():
        start(r + 1, 1 - slot)

    def wait_one(p, carry):
        page_copy(r, slot, p).wait()
        return carry

    lax.fori_loop(0, pages_of(r), wait_one, 0)
    kv = kvbuf.at[slot]
    keys = kv[:, :, :half].reshape(MAXLEN, half)
    values = kv[:, :, half:].reshape(MAXLEN, half)
    q = q_ref[0]
    scores = lax.dot_general(
        q, keys, (((1,), (1,)), ((), ())), preferred_element_type=jnp.float32
    ) * (1.0 / math.sqrt(HEAD))
    valid = lax.broadcasted_iota(jnp.int32, scores.shape, 1) < lengths[r]
    masked = jnp.where(valid, scores, -1e30)
    top = jnp.max(masked, axis=1, keepdims=True)
    expos = jnp.where(valid, jnp.exp(masked - top), 0.0)
    total = jnp.sum(expos, axis=1, keepdims=True)
    mix = jnp.dot(expos.astype(jnp.bfloat16), values, preferred_element_type=jnp.float32)
    max_ref[0] = jnp.broadcast_to(top, max_ref.shape[1:])
    tot_ref[0] = jnp.broadcast_to(total, tot_ref.shape[1:])
    mix_ref[0] = mix


def paged_attend(query_rows, tables, lengths, pool):
    count = query_rows.shape[0]
    group_size = HEADS // KV_HEADS
    half = KV_HEADS * HEAD
    heads = query_rows.reshape(count, KV_HEADS, group_size, 1, HEAD)
    mask = (jnp.arange(KV_HEADS)[:, None] == jnp.arange(KV_HEADS)[None, :])
    spread = jnp.where(
        mask[None, :, None, :, None], heads, jnp.zeros((), query_rows.dtype)
    ).reshape(count, HEADS, half)
    kv_width = pool.shape[2]
    grid_spec = pltpu.PrefetchScalarGridSpec(
        num_scalar_prefetch=2,
        grid=(count,),
        in_specs=[
            pl.BlockSpec((1, HEADS, half), lambda r, t, l: (r, 0, 0)),
            pl.BlockSpec(memory_space=pl.ANY),
        ],
        out_specs=[
            pl.BlockSpec((1, HEADS, 128), lambda r, t, l: (r, 0, 0)),
            pl.BlockSpec((1, HEADS, 128), lambda r, t, l: (r, 0, 0)),
            pl.BlockSpec((1, HEADS, half), lambda r, t, l: (r, 0, 0)),
        ],
        scratch_shapes=[
            pltpu.VMEM((2, NPAGE, PAGE, kv_width), pool.dtype),
            pltpu.SemaphoreType.DMA((2, NPAGE)),
        ],
    )
    top, total, mix = pl.pallas_call(
        attend_kernel,
        grid_spec=grid_spec,
        out_shape=[
            jax.ShapeDtypeStruct((count, HEADS, 128), jnp.float32),
            jax.ShapeDtypeStruct((count, HEADS, 128), jnp.float32),
            jax.ShapeDtypeStruct((count, HEADS, half), jnp.float32),
        ],
        compiler_params=pltpu.CompilerParams(dimension_semantics=("arbitrary",)),
        cost_estimate=pl.CostEstimate(
            flops=count * 4 * HEADS * MAXLEN * half,
            transcendentals=count * HEADS * MAXLEN,
            bytes_accessed=count * MAXLEN * kv_width * 2,
        ),
    )(tables, lengths, spread, pool)
    blocks = mix.reshape(count, KV_HEADS, group_size, KV_HEADS, HEAD)
    mixture = jnp.sum(jnp.where(mask[None, :, None, :, None], blocks, 0.0), axis=3)
    return (
        top[:, :, 0].reshape(count, KV_HEADS, group_size),
        total[:, :, 0].reshape(count, KV_HEADS, group_size),
        mixture,
    )


def in_one_piece(arrays, axis, split_dim, concat_dim, along):
    columns = [a.reshape(*a.shape[:along], -1) for a in arrays]
    both = jnp.concatenate(columns, axis=along)
    result, at, gathered = (
        lax.all_to_all(both, axis, split_axis=split_dim, concat_axis=concat_dim, tiled=True),
        0,
        [],
    )
    for a, column in zip(arrays, columns):
        share = result[..., at : at + column.shape[along]]
        gathered.append(share.reshape(*share.shape[:along], *a.shape[along:]))
        at += column.shape[along]
    return tuple(gathered)


def side_by_side(arrays, axis, dim, along):
    widths = [math.prod(a.shape[along:]) for a in arrays]
    both = jnp.concatenate(
        [a.reshape(*a.shape[:along], w) for a, w in zip(arrays, widths)], axis=along
    )
    result = lax.all_gather(both, axis, axis=dim, tiled=True)
    blocks = jnp.split(result, [sum(widths[:k]) for k in range(1, len(widths))], axis=along)
    return tuple(
        (b.reshape(*result.shape[:along], *a.shape[along:]) for a, b in zip(arrays, blocks))
    )


def partial_attend(query_heads, keyval, lengths):
    count_req, positions, kv_width = keyval.shape
    kv_count = query_heads.shape[1]
    head_size = query_heads.shape[3]
    half_width = kv_count * head_size
    key_rows = keyval[:, :, :half_width].reshape(count_req, positions, kv_count, head_size)
    value_rows = keyval[:, :, half_width:].reshape(count_req, positions, kv_count, head_size)
    scores = jnp.einsum(
        "nkgh,ntkh->nkgt", query_heads, key_rows, preferred_element_type=jnp.float32
    ) * (1.0 / math.sqrt(head_size))
    valid = (jnp.arange(positions)[None, :] < lengths[:, None])[:, None, None, :]
    masked = jnp.where(valid, scores, -1e30)
    cache_max = jnp.max(masked, axis=3)
    expos = jnp.where(valid, jnp.exp(masked - cache_max[..., None]), 0.0)
    totals = jnp.sum(expos, axis=3)
    weights = expos.astype(jnp.bfloat16)
    mixture = jnp.einsum("nkgt,ntkh->nkgh", weights, value_rows, preferred_element_type=jnp.float32)
    return (cache_max, totals, mixture)


def finish(query_heads, fresh, cache_max, totals, mixture):
    count_req, kv_count, group_size, head_size = query_heads.shape
    half_width = kv_count * head_size
    own_key = fresh[:, :half_width].reshape(count_req, kv_count, head_size)
    own_value = fresh[:, half_width:].reshape(count_req, kv_count, head_size).astype(jnp.float32)
    own_score = jnp.einsum(
        "nkgh,nkh->nkg", query_heads, own_key, preferred_element_type=jnp.float32
    ) * (1.0 / math.sqrt(head_size))
    highest = jnp.maximum(cache_max, own_score)
    old_share = jnp.exp(cache_max - highest)
    new_share = jnp.exp(own_score - highest)
    weighted = old_share[..., None] * mixture + new_share[..., None] * own_value[:, :, None, :]
    output = weighted / (old_share * totals + new_share)[..., None]
    return output.reshape(count_req, kv_count * group_size * head_size).astype(jnp.bfloat16)


def body(
    queries,
    new_kv,
    cache_pool,
    cache_len,
    local_pages,
    anchor,
    push_pages,
    prefill_attn,
    residual,
    out_weight,
    norm_gain,
    router,
    routes,
    gate_up,
    down_proj,
):
    columns = lax.axis_size("gy")
    slot_count = (MOVED + columns - 2) // (columns - 1)
    group_size = HEADS // KV_HEADS
    kv_width = 2 * KV_HEADS * HEAD
    query_heads = queries.reshape(R_DEV, KV_HEADS, group_size, HEAD)
    matches = (anchor[:, None] == jnp.arange(columns, dtype=jnp.int32)[None, :]).astype(jnp.int32)
    earlier = jnp.sum((jnp.cumsum(matches, axis=0) - 1) * matches, axis=1)
    chosen = anchor * slot_count + earlier
    local_max, local_totals, local_mix = paged_attend(
        queries[:LOCAL], local_pages, cache_len[:LOCAL], cache_pool
    )
    picker = chosen[:, None] == jnp.arange(columns * slot_count, dtype=jnp.int32)[None, :]
    sent_queries = jnp.einsum(
        "ms,md->sd",
        picker.astype(jnp.bfloat16),
        queries[LOCAL:],
        preferred_element_type=jnp.float32,
    )
    sent_lengths = jnp.sum(
        jnp.where(picker, cache_len[LOCAL:, None].astype(jnp.float32), 0.0), axis=0
    )
    got_queries, got_lengths = in_one_piece(
        (sent_queries.reshape(columns, slot_count, D), sent_lengths.reshape(columns, slot_count)),
        "gy",
        0,
        0,
        2,
    )
    far_max, far_totals, far_mix = paged_attend(
        got_queries.astype(jnp.bfloat16).reshape(columns * slot_count, D),
        push_pages,
        got_lengths.reshape(columns * slot_count).astype(jnp.int32),
        cache_pool,
    )
    back_max, back_totals, back_mix = in_one_piece(
        (
            far_max.reshape(columns, slot_count, KV_HEADS, group_size),
            far_totals.reshape(columns, slot_count, KV_HEADS, group_size),
            far_mix.reshape(columns, slot_count, KV_HEADS, group_size, HEAD),
        ),
        "gy",
        0,
        0,
        4,
    )
    cache_max = jnp.concatenate(
        [local_max, back_max.reshape(columns * slot_count, KV_HEADS, group_size)[chosen]], axis=0
    )
    totals = jnp.concatenate(
        [local_totals, back_totals.reshape(columns * slot_count, KV_HEADS, group_size)[chosen]],
        axis=0,
    )
    mixture = jnp.concatenate(
        [local_mix, back_mix.reshape(columns * slot_count, KV_HEADS, group_size, HEAD)[chosen]],
        axis=0,
    )
    attended = finish(query_heads, new_kv, cache_max, totals, mixture)
    tokens = jnp.concatenate([attended, prefill_attn], axis=0)
    row_count = tokens.shape[0]
    full_out = lax.all_gather(out_weight, "gx", axis=0, tiled=True)
    full_pair = lax.all_gather(gate_up, "gx", axis=0, tiled=True)
    full_down = lax.all_gather(down_proj, "gx", axis=0, tiled=True)
    stream = residual.astype(jnp.float32) + jnp.dot(
        tokens, full_out, preferred_element_type=jnp.float32
    )
    normed = (
        stream
        * lax.rsqrt(jnp.mean(stream * stream, axis=1, keepdims=True) + 1e-06)
        * norm_gain.astype(jnp.float32)
    ).astype(jnp.bfloat16)
    logits = jnp.dot(normed, router, preferred_element_type=jnp.float32)
    selector = routes[:, :, None] == jnp.arange(EXPERTS, dtype=jnp.int32)[None, None, :]
    gate_weights = jax.nn.softmax(
        jnp.sum(jnp.where(selector, logits[:, None, :], 0.0), axis=2), axis=1
    )
    row_hits = jnp.any(selector, axis=1)
    earlier_rows = (
        lax.broadcasted_iota(jnp.int32, (row_count, row_count), 1)
        < lax.broadcasted_iota(jnp.int32, (row_count, row_count), 0)
    ).astype(jnp.bfloat16)
    counts = jnp.dot(
        earlier_rows, row_hits.astype(jnp.bfloat16), preferred_element_type=jnp.float32
    ).astype(jnp.int32)
    place_of = jnp.sum(jnp.where(selector, counts[:, None, :], 0), axis=2)
    experts_dev = full_pair.shape[1]
    slot_hits = row_hits.T[:, None, :] & (
        counts.T[:, None, :] == jnp.arange(CAP, dtype=jnp.int32)[None, :, None]
    )
    chunk_hits = slot_hits.reshape(columns, experts_dev, CAP, row_count)
    returned_parts = []
    for local in range(experts_dev):
        outgoing = jnp.einsum(
            "scr,rd->scd",
            chunk_hits[:, local].astype(jnp.bfloat16),
            normed,
            preferred_element_type=jnp.float32,
        ).astype(jnp.bfloat16)
        arrived = lax.all_to_all(outgoing, "gy", split_axis=0, concat_axis=0, tiled=True)
        gate_pair = jnp.einsum(
            "scd,df->scf", arrived, full_pair[:, local], preferred_element_type=jnp.float32
        )
        hidden = (jax.nn.silu(gate_pair[..., :FF]) * gate_pair[..., FF:]).astype(jnp.bfloat16)
        expert_rows = jnp.einsum(
            "scf,df->scd", hidden, full_down[:, local], preferred_element_type=jnp.float32
        ).astype(jnp.bfloat16)
        returned_parts.append(
            lax.all_to_all(expert_rows, "gy", split_axis=0, concat_axis=0, tiled=True)
        )
    flat_place = place_of.reshape(row_count * TOP)
    flat_expert = routes.reshape(row_count * TOP)
    picked = None
    for local, part in enumerate(returned_parts):
        spot = jnp.where(
            flat_expert % experts_dev == local, flat_expert // experts_dev * CAP + flat_place, -1
        )
        one_hot = (spot[:, None] == jnp.arange(columns * CAP, dtype=jnp.int32)[None, :]).astype(
            jnp.bfloat16
        )
        share = jnp.dot(
            one_hot, part.reshape(columns * CAP, D), preferred_element_type=jnp.float32
        )
        picked = share if picked is None else picked + share
    picked = picked.reshape(row_count, TOP, D)
    layer_out = stream + jnp.sum(gate_weights[:, :, None] * picked, axis=1)
    return (attended, layer_out)


def solution(mesh):
    placed = (
        P(("gx", "gy"), None),
        P(("gx", "gy"), None),
        P(("gx", "gy"), None, None),
        P(("gx", "gy")),
        P(("gx", "gy"), None),
        P(("gx", "gy")),
        P(("gx", "gy"), None),
        P(("gx", "gy"), None),
        P(("gx", "gy"), None),
        P("gx", None),
        P(),
        P(),
        P(("gx", "gy"), None),
        P("gx", "gy", None),
        P("gx", "gy", None),
    )
    return jax.shard_map(
        body,
        mesh=mesh,
        in_specs=placed,
        out_specs=(P(("gx", "gy"), None), P(("gx", "gy"), None)),
        check_vma=False,
    )
```

```python
import math

import jax
import jax.numpy as jnp
from jax import lax
from jax.sharding import PartitionSpec as P
from jax.experimental import pallas as pl
from jax.experimental.pallas import tpu as pltpu

D = 1536
HEADS = 24
KV_HEADS = 8
HEAD = 64
EXPERTS = 32
FF = 512
TOP = 8
MAXLEN = 512
R_DEV = 16
LOCAL = 8
MOVED = 8
CAP = 48
NPAGE = 32
PAGE = 16


def attend_kernel(tables, lengths, q_ref, pool_ref, max_ref, tot_ref, mix_ref, kvbuf, sems):
    r = pl.program_id(0)
    n = pl.num_programs(0)
    half = KV_HEADS * HEAD

    def pages_of(req):
        return (lengths[req] + PAGE - 1) // PAGE

    def page_copy(req, slot, p):
        return pltpu.make_async_copy(
            pool_ref.at[tables[req, p]], kvbuf.at[slot, p], sems.at[slot, p]
        )

    def start(req, slot):
        def one(p, carry):
            page_copy(req, slot, p).start()
            return carry

        lax.fori_loop(0, pages_of(req), one, 0)

    @pl.when(r == 0)
    def _():
        kvbuf[...] = jnp.zeros(kvbuf.shape, kvbuf.dtype)
        start(0, 0)

    slot = r % 2

    @pl.when(r + 1 < n)
    def _():
        start(r + 1, 1 - slot)

    def wait_one(p, carry):
        page_copy(r, slot, p).wait()
        return carry

    lax.fori_loop(0, pages_of(r), wait_one, 0)
    kv = kvbuf.at[slot]
    keys = kv[:, :, :half].reshape(MAXLEN, half)
    values = kv[:, :, half:].reshape(MAXLEN, half)
    q = q_ref[0]
    scores = lax.dot_general(
        q, keys, (((1,), (1,)), ((), ())), preferred_element_type=jnp.float32
    ) * (1.0 / math.sqrt(HEAD))
    valid = lax.broadcasted_iota(jnp.int32, scores.shape, 1) < lengths[r]
    masked = jnp.where(valid, scores, -1e30)
    top = jnp.max(masked, axis=1, keepdims=True)
    expos = jnp.where(valid, jnp.exp(masked - top), 0.0)
    total = jnp.sum(expos, axis=1, keepdims=True)
    mix = jnp.dot(expos.astype(jnp.bfloat16), values, preferred_element_type=jnp.float32)
    max_ref[0] = jnp.broadcast_to(top, max_ref.shape[1:])
    tot_ref[0] = jnp.broadcast_to(total, tot_ref.shape[1:])
    mix_ref[0] = mix


def exchange_kernel(x_ref, y_ref, send_sems, recv_sems, own_sem):
    n = x_ref.shape[0]
    me = lax.axis_index("gy")
    row = lax.axis_index("gx")
    mesh_ids = pl.DeviceIdType.MESH
    barrier = pltpu.get_barrier_semaphore()
    for k in range(1, n):
        pl.semaphore_signal(
            barrier, inc=1, device_id=(row, lax.rem(me + k, n)), device_id_type=mesh_ids
        )
    pl.semaphore_wait(barrier, n - 1)
    own = pltpu.make_async_copy(x_ref.at[me], y_ref.at[me], own_sem)
    own.start()
    copies = []
    for k in range(1, n):
        dest = lax.rem(me + k, n)
        copy = pltpu.make_async_remote_copy(
            src_ref=x_ref.at[dest],
            dst_ref=y_ref.at[me],
            send_sem=send_sems.at[k],
            recv_sem=recv_sems.at[k],
            device_id=(row, dest),
            device_id_type=mesh_ids,
        )
        copy.start()
        copies.append(copy)
    for k in range(1, n):
        source = lax.rem(me + n - k, n)
        pltpu.make_async_remote_copy(
            src_ref=x_ref.at[source],
            dst_ref=y_ref.at[source],
            send_sem=send_sems.at[k],
            recv_sem=recv_sems.at[k],
            device_id=(row, source),
            device_id_type=mesh_ids,
        ).wait_recv()
    for copy in copies:
        copy.wait_send()
    own.wait()


def exchange(x, tag):
    n = x.shape[0]
    block = x.size // n * x.dtype.itemsize
    return pl.pallas_call(
        exchange_kernel,
        out_shape=jax.ShapeDtypeStruct(x.shape, x.dtype),
        in_specs=[pl.BlockSpec(memory_space=pl.ANY)],
        out_specs=pl.BlockSpec(memory_space=pl.ANY),
        scratch_shapes=[
            pltpu.SemaphoreType.DMA((n,)),
            pltpu.SemaphoreType.DMA((n,)),
            pltpu.SemaphoreType.DMA,
        ],
        compiler_params=pltpu.CompilerParams(collective_id=tag, has_side_effects=True),
        cost_estimate=pl.CostEstimate(
            flops=0, transcendentals=0, bytes_accessed=2 * n * block
        ),
    )(x)


def paged_attend(query_rows, tables, lengths, pool):
    count = query_rows.shape[0]
    group_size = HEADS // KV_HEADS
    half = KV_HEADS * HEAD
    heads = query_rows.reshape(count, KV_HEADS, group_size, 1, HEAD)
    mask = (jnp.arange(KV_HEADS)[:, None] == jnp.arange(KV_HEADS)[None, :])
    spread = jnp.where(
        mask[None, :, None, :, None], heads, jnp.zeros((), query_rows.dtype)
    ).reshape(count, HEADS, half)
    kv_width = pool.shape[2]
    grid_spec = pltpu.PrefetchScalarGridSpec(
        num_scalar_prefetch=2,
        grid=(count,),
        in_specs=[
            pl.BlockSpec((1, HEADS, half), lambda r, t, l: (r, 0, 0)),
            pl.BlockSpec(memory_space=pl.ANY),
        ],
        out_specs=[
            pl.BlockSpec((1, HEADS, 128), lambda r, t, l: (r, 0, 0)),
            pl.BlockSpec((1, HEADS, 128), lambda r, t, l: (r, 0, 0)),
            pl.BlockSpec((1, HEADS, half), lambda r, t, l: (r, 0, 0)),
        ],
        scratch_shapes=[
            pltpu.VMEM((2, NPAGE, PAGE, kv_width), pool.dtype),
            pltpu.SemaphoreType.DMA((2, NPAGE)),
        ],
    )
    top, total, mix = pl.pallas_call(
        attend_kernel,
        grid_spec=grid_spec,
        out_shape=[
            jax.ShapeDtypeStruct((count, HEADS, 128), jnp.float32),
            jax.ShapeDtypeStruct((count, HEADS, 128), jnp.float32),
            jax.ShapeDtypeStruct((count, HEADS, half), jnp.float32),
        ],
        compiler_params=pltpu.CompilerParams(dimension_semantics=("arbitrary",)),
        cost_estimate=pl.CostEstimate(
            flops=count * 4 * HEADS * MAXLEN * half,
            transcendentals=count * HEADS * MAXLEN,
            bytes_accessed=count * MAXLEN * kv_width * 2,
        ),
    )(tables, lengths, spread, pool)
    blocks = mix.reshape(count, KV_HEADS, group_size, KV_HEADS, HEAD)
    mixture = jnp.sum(jnp.where(mask[None, :, None, :, None], blocks, 0.0), axis=3)
    return (
        top[:, :, 0].reshape(count, KV_HEADS, group_size),
        total[:, :, 0].reshape(count, KV_HEADS, group_size),
        mixture,
    )


def in_one_piece(arrays, tag, along):
    columns = [a.reshape(*a.shape[:along], -1) for a in arrays]
    both = jnp.concatenate(columns, axis=along)
    result, at, gathered = (exchange(both, tag), 0, [])
    for a, column in zip(arrays, columns):
        share = result[..., at : at + column.shape[along]]
        gathered.append(share.reshape(*share.shape[:along], *a.shape[along:]))
        at += column.shape[along]
    return tuple(gathered)


def side_by_side(arrays, axis, dim, along):
    widths = [math.prod(a.shape[along:]) for a in arrays]
    both = jnp.concatenate(
        [a.reshape(*a.shape[:along], w) for a, w in zip(arrays, widths)], axis=along
    )
    result = lax.all_gather(both, axis, axis=dim, tiled=True)
    blocks = jnp.split(result, [sum(widths[:k]) for k in range(1, len(widths))], axis=along)
    return tuple(
        (b.reshape(*result.shape[:along], *a.shape[along:]) for a, b in zip(arrays, blocks))
    )


def partial_attend(query_heads, keyval, lengths):
    count_req, positions, kv_width = keyval.shape
    kv_count = query_heads.shape[1]
    head_size = query_heads.shape[3]
    half_width = kv_count * head_size
    key_rows = keyval[:, :, :half_width].reshape(count_req, positions, kv_count, head_size)
    value_rows = keyval[:, :, half_width:].reshape(count_req, positions, kv_count, head_size)
    scores = jnp.einsum(
        "nkgh,ntkh->nkgt", query_heads, key_rows, preferred_element_type=jnp.float32
    ) * (1.0 / math.sqrt(head_size))
    valid = (jnp.arange(positions)[None, :] < lengths[:, None])[:, None, None, :]
    masked = jnp.where(valid, scores, -1e30)
    cache_max = jnp.max(masked, axis=3)
    expos = jnp.where(valid, jnp.exp(masked - cache_max[..., None]), 0.0)
    totals = jnp.sum(expos, axis=3)
    weights = expos.astype(jnp.bfloat16)
    mixture = jnp.einsum("nkgt,ntkh->nkgh", weights, value_rows, preferred_element_type=jnp.float32)
    return (cache_max, totals, mixture)


def finish(query_heads, fresh, cache_max, totals, mixture):
    count_req, kv_count, group_size, head_size = query_heads.shape
    half_width = kv_count * head_size
    own_key = fresh[:, :half_width].reshape(count_req, kv_count, head_size)
    own_value = fresh[:, half_width:].reshape(count_req, kv_count, head_size).astype(jnp.float32)
    own_score = jnp.einsum(
        "nkgh,nkh->nkg", query_heads, own_key, preferred_element_type=jnp.float32
    ) * (1.0 / math.sqrt(head_size))
    highest = jnp.maximum(cache_max, own_score)
    old_share = jnp.exp(cache_max - highest)
    new_share = jnp.exp(own_score - highest)
    weighted = old_share[..., None] * mixture + new_share[..., None] * own_value[:, :, None, :]
    output = weighted / (old_share * totals + new_share)[..., None]
    return output.reshape(count_req, kv_count * group_size * head_size).astype(jnp.bfloat16)


def body(
    queries,
    new_kv,
    cache_pool,
    cache_len,
    local_pages,
    anchor,
    push_pages,
    prefill_attn,
    residual,
    out_weight,
    norm_gain,
    router,
    routes,
    gate_up,
    down_proj,
):
    columns = lax.axis_size("gy")
    slot_count = (MOVED + columns - 2) // (columns - 1)
    group_size = HEADS // KV_HEADS
    kv_width = 2 * KV_HEADS * HEAD
    query_heads = queries.reshape(R_DEV, KV_HEADS, group_size, HEAD)
    matches = (anchor[:, None] == jnp.arange(columns, dtype=jnp.int32)[None, :]).astype(jnp.int32)
    earlier = jnp.sum((jnp.cumsum(matches, axis=0) - 1) * matches, axis=1)
    chosen = anchor * slot_count + earlier
    local_max, local_totals, local_mix = paged_attend(
        queries[:LOCAL], local_pages, cache_len[:LOCAL], cache_pool
    )
    picker = chosen[:, None] == jnp.arange(columns * slot_count, dtype=jnp.int32)[None, :]
    sent_queries = jnp.einsum(
        "ms,md->sd",
        picker.astype(jnp.bfloat16),
        queries[LOCAL:],
        preferred_element_type=jnp.float32,
    )
    sent_lengths = jnp.sum(
        jnp.where(picker, cache_len[LOCAL:, None].astype(jnp.float32), 0.0), axis=0
    )
    got_queries, got_lengths = in_one_piece(
        (sent_queries.reshape(columns, slot_count, D), sent_lengths.reshape(columns, slot_count)),
        3,
        2,
    )
    far_max, far_totals, far_mix = paged_attend(
        got_queries.astype(jnp.bfloat16).reshape(columns * slot_count, D),
        push_pages,
        got_lengths.reshape(columns * slot_count).astype(jnp.int32),
        cache_pool,
    )
    back_max, back_totals, back_mix = in_one_piece(
        (
            far_max.reshape(columns, slot_count, KV_HEADS, group_size),
            far_totals.reshape(columns, slot_count, KV_HEADS, group_size),
            far_mix.reshape(columns, slot_count, KV_HEADS, group_size, HEAD),
        ),
        4,
        4,
    )
    cache_max = jnp.concatenate(
        [local_max, back_max.reshape(columns * slot_count, KV_HEADS, group_size)[chosen]], axis=0
    )
    totals = jnp.concatenate(
        [local_totals, back_totals.reshape(columns * slot_count, KV_HEADS, group_size)[chosen]],
        axis=0,
    )
    mixture = jnp.concatenate(
        [local_mix, back_mix.reshape(columns * slot_count, KV_HEADS, group_size, HEAD)[chosen]],
        axis=0,
    )
    attended = finish(query_heads, new_kv, cache_max, totals, mixture)
    tokens = jnp.concatenate([attended, prefill_attn], axis=0)
    row_count = tokens.shape[0]
    full_out = lax.all_gather(out_weight, "gx", axis=0, tiled=True)
    full_pair = lax.all_gather(gate_up, "gx", axis=0, tiled=True)
    full_down = lax.all_gather(down_proj, "gx", axis=0, tiled=True)
    stream = residual.astype(jnp.float32) + jnp.dot(
        tokens, full_out, preferred_element_type=jnp.float32
    )
    normed = (
        stream
        * lax.rsqrt(jnp.mean(stream * stream, axis=1, keepdims=True) + 1e-06)
        * norm_gain.astype(jnp.float32)
    ).astype(jnp.bfloat16)
    logits = jnp.dot(normed, router, preferred_element_type=jnp.float32)
    selector = routes[:, :, None] == jnp.arange(EXPERTS, dtype=jnp.int32)[None, None, :]
    gate_weights = jax.nn.softmax(
        jnp.sum(jnp.where(selector, logits[:, None, :], 0.0), axis=2), axis=1
    )
    row_hits = jnp.any(selector, axis=1)
    earlier_rows = (
        lax.broadcasted_iota(jnp.int32, (row_count, row_count), 1)
        < lax.broadcasted_iota(jnp.int32, (row_count, row_count), 0)
    ).astype(jnp.bfloat16)
    counts = jnp.dot(
        earlier_rows, row_hits.astype(jnp.bfloat16), preferred_element_type=jnp.float32
    ).astype(jnp.int32)
    place_of = jnp.sum(jnp.where(selector, counts[:, None, :], 0), axis=2)
    experts_dev = full_pair.shape[1]
    slot_hits = row_hits.T[:, None, :] & (
        counts.T[:, None, :] == jnp.arange(CAP, dtype=jnp.int32)[None, :, None]
    )
    chunk_hits = slot_hits.reshape(columns, experts_dev, CAP, row_count)
    returned_parts = []
    for local in range(experts_dev):
        outgoing = jnp.einsum(
            "scr,rd->scd",
            chunk_hits[:, local].astype(jnp.bfloat16),
            normed,
            preferred_element_type=jnp.float32,
        ).astype(jnp.bfloat16)
        arrived = lax.all_to_all(outgoing, "gy", split_axis=0, concat_axis=0, tiled=True)
        gate_pair = jnp.einsum(
            "scd,df->scf", arrived, full_pair[:, local], preferred_element_type=jnp.float32
        )
        hidden = (jax.nn.silu(gate_pair[..., :FF]) * gate_pair[..., FF:]).astype(jnp.bfloat16)
        expert_rows = jnp.einsum(
            "scf,df->scd", hidden, full_down[:, local], preferred_element_type=jnp.float32
        ).astype(jnp.bfloat16)
        returned_parts.append(
            lax.all_to_all(expert_rows, "gy", split_axis=0, concat_axis=0, tiled=True)
        )
    flat_place = place_of.reshape(row_count * TOP)
    flat_expert = routes.reshape(row_count * TOP)
    picked = None
    for local, part in enumerate(returned_parts):
        spot = jnp.where(
            flat_expert % experts_dev == local, flat_expert // experts_dev * CAP + flat_place, -1
        )
        one_hot = (spot[:, None] == jnp.arange(columns * CAP, dtype=jnp.int32)[None, :]).astype(
            jnp.bfloat16
        )
        share = jnp.dot(
            one_hot, part.reshape(columns * CAP, D), preferred_element_type=jnp.float32
        )
        picked = share if picked is None else picked + share
    picked = picked.reshape(row_count, TOP, D)
    layer_out = stream + jnp.sum(gate_weights[:, :, None] * picked, axis=1)
    return (attended, layer_out)


def solution(mesh):
    placed = (
        P(("gx", "gy"), None),
        P(("gx", "gy"), None),
        P(("gx", "gy"), None, None),
        P(("gx", "gy")),
        P(("gx", "gy"), None),
        P(("gx", "gy")),
        P(("gx", "gy"), None),
        P(("gx", "gy"), None),
        P(("gx", "gy"), None),
        P("gx", None),
        P(),
        P(),
        P(("gx", "gy"), None),
        P("gx", "gy", None),
        P("gx", "gy", None),
    )
    return jax.shard_map(
        body,
        mesh=mesh,
        in_specs=placed,
        out_specs=(P(("gx", "gy"), None), P(("gx", "gy"), None)),
        check_vma=False,
    )
```

```python
import math

import jax
import jax.numpy as jnp
from jax import lax
from jax.sharding import PartitionSpec as P
from jax.experimental import pallas as pl
from jax.experimental.pallas import tpu as pltpu

D = 1536
HEADS = 24
KV_HEADS = 8
HEAD = 64
EXPERTS = 32
FF = 512
TOP = 8
MAXLEN = 512
R_DEV = 16
LOCAL = 8
MOVED = 8
CAP = 48
NPAGE = 32
PAGE = 16


def attend_kernel(tables, lengths, q_ref, pool_ref, max_ref, tot_ref, mix_ref, kvbuf, sems):
    r = pl.program_id(0)
    n = pl.num_programs(0)
    half = KV_HEADS * HEAD

    def pages_of(req):
        return (lengths[req] + PAGE - 1) // PAGE

    def page_copy(req, slot, p):
        return pltpu.make_async_copy(
            pool_ref.at[tables[req, p]], kvbuf.at[slot, p], sems.at[slot, p]
        )

    def start(req, slot):
        def one(p, carry):
            page_copy(req, slot, p).start()
            return carry

        lax.fori_loop(0, pages_of(req), one, 0)

    @pl.when(r == 0)
    def _():
        kvbuf[...] = jnp.zeros(kvbuf.shape, kvbuf.dtype)
        start(0, 0)

    slot = r % 2

    @pl.when(r + 1 < n)
    def _():
        start(r + 1, 1 - slot)

    def wait_one(p, carry):
        page_copy(r, slot, p).wait()
        return carry

    lax.fori_loop(0, pages_of(r), wait_one, 0)
    kv = kvbuf.at[slot]
    keys = kv[:, :, :half].reshape(MAXLEN, half)
    values = kv[:, :, half:].reshape(MAXLEN, half)
    q = q_ref[0]
    scores = lax.dot_general(
        q, keys, (((1,), (1,)), ((), ())), preferred_element_type=jnp.float32
    ) * (1.0 / math.sqrt(HEAD))
    valid = lax.broadcasted_iota(jnp.int32, scores.shape, 1) < lengths[r]
    masked = jnp.where(valid, scores, -1e30)
    top = jnp.max(masked, axis=1, keepdims=True)
    expos = jnp.where(valid, jnp.exp(masked - top), 0.0)
    total = jnp.sum(expos, axis=1, keepdims=True)
    mix = jnp.dot(expos.astype(jnp.bfloat16), values, preferred_element_type=jnp.float32)
    max_ref[0] = jnp.broadcast_to(top, max_ref.shape[1:])
    tot_ref[0] = jnp.broadcast_to(total, tot_ref.shape[1:])
    mix_ref[0] = mix


def paged_attend(query_rows, tables, lengths, pool):
    count = query_rows.shape[0]
    group_size = HEADS // KV_HEADS
    half = KV_HEADS * HEAD
    heads = query_rows.reshape(count, KV_HEADS, group_size, 1, HEAD)
    mask = (jnp.arange(KV_HEADS)[:, None] == jnp.arange(KV_HEADS)[None, :])
    spread = jnp.where(
        mask[None, :, None, :, None], heads, jnp.zeros((), query_rows.dtype)
    ).reshape(count, HEADS, half)
    kv_width = pool.shape[2]
    grid_spec = pltpu.PrefetchScalarGridSpec(
        num_scalar_prefetch=2,
        grid=(count,),
        in_specs=[
            pl.BlockSpec((1, HEADS, half), lambda r, t, l: (r, 0, 0)),
            pl.BlockSpec(memory_space=pl.ANY),
        ],
        out_specs=[
            pl.BlockSpec((1, HEADS, 128), lambda r, t, l: (r, 0, 0)),
            pl.BlockSpec((1, HEADS, 128), lambda r, t, l: (r, 0, 0)),
            pl.BlockSpec((1, HEADS, half), lambda r, t, l: (r, 0, 0)),
        ],
        scratch_shapes=[
            pltpu.VMEM((2, NPAGE, PAGE, kv_width), pool.dtype),
            pltpu.SemaphoreType.DMA((2, NPAGE)),
        ],
    )
    top, total, mix = pl.pallas_call(
        attend_kernel,
        grid_spec=grid_spec,
        out_shape=[
            jax.ShapeDtypeStruct((count, HEADS, 128), jnp.float32),
            jax.ShapeDtypeStruct((count, HEADS, 128), jnp.float32),
            jax.ShapeDtypeStruct((count, HEADS, half), jnp.float32),
        ],
        compiler_params=pltpu.CompilerParams(dimension_semantics=("arbitrary",)),
        cost_estimate=pl.CostEstimate(
            flops=count * 4 * HEADS * MAXLEN * half,
            transcendentals=count * HEADS * MAXLEN,
            bytes_accessed=count * MAXLEN * kv_width * 2,
        ),
    )(tables, lengths, spread, pool)
    blocks = mix.reshape(count, KV_HEADS, group_size, KV_HEADS, HEAD)
    mixture = jnp.sum(jnp.where(mask[None, :, None, :, None], blocks, 0.0), axis=3)
    return (
        top[:, :, 0].reshape(count, KV_HEADS, group_size),
        total[:, :, 0].reshape(count, KV_HEADS, group_size),
        mixture,
    )


def in_one_piece(arrays, axis, split_dim, concat_dim, along):
    columns = [a.reshape(*a.shape[:along], -1) for a in arrays]
    both = jnp.concatenate(columns, axis=along)
    result, at, gathered = (
        lax.all_to_all(both, axis, split_axis=split_dim, concat_axis=concat_dim, tiled=True),
        0,
        [],
    )
    for a, column in zip(arrays, columns):
        share = result[..., at : at + column.shape[along]]
        gathered.append(share.reshape(*share.shape[:along], *a.shape[along:]))
        at += column.shape[along]
    return tuple(gathered)


def side_by_side(arrays, axis, dim, along):
    widths = [math.prod(a.shape[along:]) for a in arrays]
    both = jnp.concatenate(
        [a.reshape(*a.shape[:along], w) for a, w in zip(arrays, widths)], axis=along
    )
    result = lax.all_gather(both, axis, axis=dim, tiled=True)
    blocks = jnp.split(result, [sum(widths[:k]) for k in range(1, len(widths))], axis=along)
    return tuple(
        (b.reshape(*result.shape[:along], *a.shape[along:]) for a, b in zip(arrays, blocks))
    )


def partial_attend(query_heads, keyval, lengths):
    count_req, positions, kv_width = keyval.shape
    kv_count = query_heads.shape[1]
    head_size = query_heads.shape[3]
    half_width = kv_count * head_size
    key_rows = keyval[:, :, :half_width].reshape(count_req, positions, kv_count, head_size)
    value_rows = keyval[:, :, half_width:].reshape(count_req, positions, kv_count, head_size)
    scores = jnp.einsum(
        "nkgh,ntkh->nkgt", query_heads, key_rows, preferred_element_type=jnp.float32
    ) * (1.0 / math.sqrt(head_size))
    valid = (jnp.arange(positions)[None, :] < lengths[:, None])[:, None, None, :]
    masked = jnp.where(valid, scores, -1e30)
    cache_max = jnp.max(masked, axis=3)
    expos = jnp.where(valid, jnp.exp(masked - cache_max[..., None]), 0.0)
    totals = jnp.sum(expos, axis=3)
    weights = expos.astype(jnp.bfloat16)
    mixture = jnp.einsum("nkgt,ntkh->nkgh", weights, value_rows, preferred_element_type=jnp.float32)
    return (cache_max, totals, mixture)


def finish(query_heads, fresh, cache_max, totals, mixture):
    count_req, kv_count, group_size, head_size = query_heads.shape
    half_width = kv_count * head_size
    own_key = fresh[:, :half_width].reshape(count_req, kv_count, head_size)
    own_value = fresh[:, half_width:].reshape(count_req, kv_count, head_size).astype(jnp.float32)
    own_score = jnp.einsum(
        "nkgh,nkh->nkg", query_heads, own_key, preferred_element_type=jnp.float32
    ) * (1.0 / math.sqrt(head_size))
    highest = jnp.maximum(cache_max, own_score)
    old_share = jnp.exp(cache_max - highest)
    new_share = jnp.exp(own_score - highest)
    weighted = old_share[..., None] * mixture + new_share[..., None] * own_value[:, :, None, :]
    output = weighted / (old_share * totals + new_share)[..., None]
    return output.reshape(count_req, kv_count * group_size * head_size).astype(jnp.bfloat16)


def body(
    queries,
    new_kv,
    cache_pool,
    cache_len,
    local_pages,
    anchor,
    push_pages,
    prefill_attn,
    residual,
    out_weight,
    norm_gain,
    router,
    routes,
    gate_up,
    down_proj,
):
    columns = lax.axis_size("gy")
    slot_count = (MOVED + columns - 2) // (columns - 1)
    group_size = HEADS // KV_HEADS
    kv_width = 2 * KV_HEADS * HEAD
    query_heads = queries.reshape(R_DEV, KV_HEADS, group_size, HEAD)
    matches = (anchor[:, None] == jnp.arange(columns, dtype=jnp.int32)[None, :]).astype(jnp.int32)
    earlier = jnp.sum((jnp.cumsum(matches, axis=0) - 1) * matches, axis=1)
    chosen = anchor * slot_count + earlier
    local_max, local_totals, local_mix = paged_attend(
        queries[:LOCAL], local_pages, cache_len[:LOCAL], cache_pool
    )
    picker = chosen[:, None] == jnp.arange(columns * slot_count, dtype=jnp.int32)[None, :]
    sent_queries = jnp.einsum(
        "ms,md->sd",
        picker.astype(jnp.bfloat16),
        queries[LOCAL:],
        preferred_element_type=jnp.float32,
    )
    sent_lengths = jnp.sum(
        jnp.where(picker, cache_len[LOCAL:, None].astype(jnp.float32), 0.0), axis=0
    )
    got_queries, got_lengths = in_one_piece(
        (sent_queries.reshape(columns, slot_count, D), sent_lengths.reshape(columns, slot_count)),
        "gy",
        0,
        0,
        2,
    )
    far_max, far_totals, far_mix = paged_attend(
        got_queries.astype(jnp.bfloat16).reshape(columns * slot_count, D),
        push_pages,
        got_lengths.reshape(columns * slot_count).astype(jnp.int32),
        cache_pool,
    )
    back_max, back_totals, back_mix = in_one_piece(
        (
            far_max.reshape(columns, slot_count, KV_HEADS, group_size),
            far_totals.reshape(columns, slot_count, KV_HEADS, group_size),
            far_mix.reshape(columns, slot_count, KV_HEADS, group_size, HEAD),
        ),
        "gy",
        0,
        0,
        4,
    )
    cache_max = jnp.concatenate(
        [local_max, back_max.reshape(columns * slot_count, KV_HEADS, group_size)[chosen]], axis=0
    )
    totals = jnp.concatenate(
        [local_totals, back_totals.reshape(columns * slot_count, KV_HEADS, group_size)[chosen]],
        axis=0,
    )
    mixture = jnp.concatenate(
        [local_mix, back_mix.reshape(columns * slot_count, KV_HEADS, group_size, HEAD)[chosen]],
        axis=0,
    )
    attended = finish(query_heads, new_kv, cache_max, totals, mixture)
    tokens = jnp.concatenate([attended, prefill_attn], axis=0)
    row_count = tokens.shape[0]
    full_out = lax.all_gather(out_weight, "gx", axis=0, tiled=True)
    full_pair = lax.all_gather(gate_up, "gx", axis=0, tiled=True)
    full_down = lax.all_gather(down_proj, "gx", axis=0, tiled=True)
    stream = residual.astype(jnp.float32) + jnp.dot(
        tokens, full_out, preferred_element_type=jnp.float32
    )
    normed = (
        stream
        * lax.rsqrt(jnp.mean(stream * stream, axis=1, keepdims=True) + 1e-06)
        * norm_gain.astype(jnp.float32)
    ).astype(jnp.bfloat16)
    logits = jnp.dot(normed, router, preferred_element_type=jnp.float32)
    selector = routes[:, :, None] == jnp.arange(EXPERTS, dtype=jnp.int32)[None, None, :]
    gate_weights = jax.nn.softmax(
        jnp.sum(jnp.where(selector, logits[:, None, :], 0.0), axis=2), axis=1
    )
    row_hits = jnp.any(selector, axis=1)
    earlier_rows = (
        lax.broadcasted_iota(jnp.int32, (row_count, row_count), 1)
        < lax.broadcasted_iota(jnp.int32, (row_count, row_count), 0)
    ).astype(jnp.bfloat16)
    counts = jnp.dot(
        earlier_rows, row_hits.astype(jnp.bfloat16), preferred_element_type=jnp.float32
    ).astype(jnp.int32)
    place_of = jnp.sum(jnp.where(selector, counts[:, None, :], 0), axis=2)
    experts_dev = full_pair.shape[1]
    slot_hits = row_hits.T[:, None, :] & (
        counts.T[:, None, :] == jnp.arange(CAP, dtype=jnp.int32)[None, :, None]
    )
    chunk_hits = slot_hits.reshape(columns, experts_dev, CAP, row_count)
    returned_parts = []
    for local in range(experts_dev):
        outgoing = jnp.einsum(
            "scr,rd->scd",
            chunk_hits[:, local].astype(jnp.bfloat16),
            normed,
            preferred_element_type=jnp.float32,
        ).astype(jnp.bfloat16)
        arrived = lax.all_to_all(outgoing, "gy", split_axis=0, concat_axis=0, tiled=True)
        gate_pair = jnp.einsum(
            "scd,df->scf", arrived, full_pair[:, local], preferred_element_type=jnp.float32
        )
        hidden = (jax.nn.silu(gate_pair[..., :FF]) * gate_pair[..., FF:]).astype(jnp.bfloat16)
        expert_rows = jnp.einsum(
            "scf,df->scd", hidden, full_down[:, local], preferred_element_type=jnp.float32
        ).astype(jnp.bfloat16)
        returned_parts.append(
            lax.all_to_all(expert_rows, "gy", split_axis=0, concat_axis=0, tiled=True)
        )
    mixed = None
    for local, part in enumerate(returned_parts):
        spot = jnp.where(routes % experts_dev == local, routes // experts_dev * CAP + place_of, -1)
        gate_spot = jnp.sum(
            jnp.where(
                spot[:, :, None] == jnp.arange(columns * CAP, dtype=jnp.int32)[None, None, :],
                gate_weights[:, :, None],
                0.0,
            ),
            axis=1,
        )
        share = jnp.dot(
            gate_spot,
            part.reshape(columns * CAP, D),
            precision=lax.Precision.HIGHEST,
            preferred_element_type=jnp.float32,
        )
        mixed = share if mixed is None else mixed + share
    layer_out = stream + mixed
    return (attended, layer_out)


def solution(mesh):
    placed = (
        P(("gx", "gy"), None),
        P(("gx", "gy"), None),
        P(("gx", "gy"), None, None),
        P(("gx", "gy")),
        P(("gx", "gy"), None),
        P(("gx", "gy")),
        P(("gx", "gy"), None),
        P(("gx", "gy"), None),
        P(("gx", "gy"), None),
        P("gx", None),
        P(),
        P(),
        P(("gx", "gy"), None),
        P("gx", "gy", None),
        P("gx", "gy", None),
    )
    return jax.shard_map(
        body,
        mesh=mesh,
        in_specs=placed,
        out_specs=(P(("gx", "gy"), None), P(("gx", "gy"), None)),
        check_vma=False,
    )
```

```python
import math

import jax
import jax.numpy as jnp
from jax import lax
from jax.sharding import PartitionSpec as P
from jax.experimental import pallas as pl
from jax.experimental.pallas import tpu as pltpu

D = 1536
HEADS = 24
KV_HEADS = 8
HEAD = 64
EXPERTS = 32
FF = 512
TOP = 8
MAXLEN = 512
R_DEV = 16
LOCAL = 8
MOVED = 8
CAP = 48
NPAGE = 32
PAGE = 16


def attend_kernel(tables, lengths, q_ref, pool_ref, max_ref, tot_ref, mix_ref, kvbuf, sems):
    r = pl.program_id(0)
    n = pl.num_programs(0)
    half = KV_HEADS * HEAD

    def pages_of(req):
        return (lengths[req] + PAGE - 1) // PAGE

    def page_copy(req, slot, p):
        return pltpu.make_async_copy(
            pool_ref.at[tables[req, p]], kvbuf.at[slot, p], sems.at[slot, p]
        )

    def start(req, slot):
        def one(p, carry):
            page_copy(req, slot, p).start()
            return carry

        lax.fori_loop(0, pages_of(req), one, 0)

    @pl.when(r == 0)
    def _():
        kvbuf[...] = jnp.zeros(kvbuf.shape, kvbuf.dtype)
        start(0, 0)

    slot = r % 2

    @pl.when(r + 1 < n)
    def _():
        start(r + 1, 1 - slot)

    def wait_one(p, carry):
        page_copy(r, slot, p).wait()
        return carry

    lax.fori_loop(0, pages_of(r), wait_one, 0)
    kv = kvbuf.at[slot]
    keys = kv[:, :, :half].reshape(MAXLEN, half)
    values = kv[:, :, half:].reshape(MAXLEN, half)
    q = q_ref[0]
    scores = jnp.dot(keys, q, preferred_element_type=jnp.float32) * (1.0 / math.sqrt(HEAD))
    valid = lax.broadcasted_iota(jnp.int32, scores.shape, 0) < lengths[r]
    masked = jnp.where(valid, scores, -1e30)
    top = jnp.max(masked, axis=0, keepdims=True)
    expos = jnp.where(valid, jnp.exp(masked - top), 0.0)
    total = jnp.sum(expos, axis=0, keepdims=True)
    mix = lax.dot_general(
        expos.astype(jnp.bfloat16),
        values,
        (((0,), (0,)), ((), ())),
        preferred_element_type=jnp.float32,
    )
    max_ref[0] = jnp.broadcast_to(top, max_ref.shape[1:])
    tot_ref[0] = jnp.broadcast_to(total, tot_ref.shape[1:])
    mix_ref[0] = mix


def paged_attend(query_rows, tables, lengths, pool):
    count = query_rows.shape[0]
    group_size = HEADS // KV_HEADS
    half = KV_HEADS * HEAD
    heads = query_rows.reshape(count, KV_HEADS, group_size, 1, HEAD)
    mask = (jnp.arange(KV_HEADS)[:, None] == jnp.arange(KV_HEADS)[None, :])
    spread = jnp.where(
        mask[None, :, None, :, None], heads, jnp.zeros((), query_rows.dtype)
    ).transpose(0, 3, 4, 1, 2).reshape(count, half, HEADS)
    kv_width = pool.shape[2]
    grid_spec = pltpu.PrefetchScalarGridSpec(
        num_scalar_prefetch=2,
        grid=(count,),
        in_specs=[
            pl.BlockSpec((1, half, HEADS), lambda r, t, l: (r, 0, 0)),
            pl.BlockSpec(memory_space=pl.ANY),
        ],
        out_specs=[
            pl.BlockSpec((1, 8, HEADS), lambda r, t, l: (r, 0, 0)),
            pl.BlockSpec((1, 8, HEADS), lambda r, t, l: (r, 0, 0)),
            pl.BlockSpec((1, HEADS, half), lambda r, t, l: (r, 0, 0)),
        ],
        scratch_shapes=[
            pltpu.VMEM((2, NPAGE, PAGE, kv_width), pool.dtype),
            pltpu.SemaphoreType.DMA((2, NPAGE)),
        ],
    )
    top, total, mix = pl.pallas_call(
        attend_kernel,
        grid_spec=grid_spec,
        out_shape=[
            jax.ShapeDtypeStruct((count, 8, HEADS), jnp.float32),
            jax.ShapeDtypeStruct((count, 8, HEADS), jnp.float32),
            jax.ShapeDtypeStruct((count, HEADS, half), jnp.float32),
        ],
        compiler_params=pltpu.CompilerParams(dimension_semantics=("arbitrary",)),
        cost_estimate=pl.CostEstimate(
            flops=count * 4 * HEADS * MAXLEN * half,
            transcendentals=count * HEADS * MAXLEN,
            bytes_accessed=count * MAXLEN * kv_width * 2,
        ),
    )(tables, lengths, spread, pool)
    blocks = mix.reshape(count, KV_HEADS, group_size, KV_HEADS, HEAD)
    mixture = jnp.sum(jnp.where(mask[None, :, None, :, None], blocks, 0.0), axis=3)
    return (
        top[:, 0, :].reshape(count, KV_HEADS, group_size),
        total[:, 0, :].reshape(count, KV_HEADS, group_size),
        mixture,
    )


def in_one_piece(arrays, axis, split_dim, concat_dim, along):
    columns = [a.reshape(*a.shape[:along], -1) for a in arrays]
    both = jnp.concatenate(columns, axis=along)
    result, at, gathered = (
        lax.all_to_all(both, axis, split_axis=split_dim, concat_axis=concat_dim, tiled=True),
        0,
        [],
    )
    for a, column in zip(arrays, columns):
        share = result[..., at : at + column.shape[along]]
        gathered.append(share.reshape(*share.shape[:along], *a.shape[along:]))
        at += column.shape[along]
    return tuple(gathered)


def side_by_side(arrays, axis, dim, along):
    widths = [math.prod(a.shape[along:]) for a in arrays]
    both = jnp.concatenate(
        [a.reshape(*a.shape[:along], w) for a, w in zip(arrays, widths)], axis=along
    )
    result = lax.all_gather(both, axis, axis=dim, tiled=True)
    blocks = jnp.split(result, [sum(widths[:k]) for k in range(1, len(widths))], axis=along)
    return tuple(
        (b.reshape(*result.shape[:along], *a.shape[along:]) for a, b in zip(arrays, blocks))
    )


def partial_attend(query_heads, keyval, lengths):
    count_req, positions, kv_width = keyval.shape
    kv_count = query_heads.shape[1]
    head_size = query_heads.shape[3]
    half_width = kv_count * head_size
    key_rows = keyval[:, :, :half_width].reshape(count_req, positions, kv_count, head_size)
    value_rows = keyval[:, :, half_width:].reshape(count_req, positions, kv_count, head_size)
    scores = jnp.einsum(
        "nkgh,ntkh->nkgt", query_heads, key_rows, preferred_element_type=jnp.float32
    ) * (1.0 / math.sqrt(head_size))
    valid = (jnp.arange(positions)[None, :] < lengths[:, None])[:, None, None, :]
    masked = jnp.where(valid, scores, -1e30)
    cache_max = jnp.max(masked, axis=3)
    expos = jnp.where(valid, jnp.exp(masked - cache_max[..., None]), 0.0)
    totals = jnp.sum(expos, axis=3)
    weights = expos.astype(jnp.bfloat16)
    mixture = jnp.einsum("nkgt,ntkh->nkgh", weights, value_rows, preferred_element_type=jnp.float32)
    return (cache_max, totals, mixture)


def finish(query_heads, fresh, cache_max, totals, mixture):
    count_req, kv_count, group_size, head_size = query_heads.shape
    half_width = kv_count * head_size
    own_key = fresh[:, :half_width].reshape(count_req, kv_count, head_size)
    own_value = fresh[:, half_width:].reshape(count_req, kv_count, head_size).astype(jnp.float32)
    own_score = jnp.einsum(
        "nkgh,nkh->nkg", query_heads, own_key, preferred_element_type=jnp.float32
    ) * (1.0 / math.sqrt(head_size))
    highest = jnp.maximum(cache_max, own_score)
    old_share = jnp.exp(cache_max - highest)
    new_share = jnp.exp(own_score - highest)
    weighted = old_share[..., None] * mixture + new_share[..., None] * own_value[:, :, None, :]
    output = weighted / (old_share * totals + new_share)[..., None]
    return output.reshape(count_req, kv_count * group_size * head_size).astype(jnp.bfloat16)


def body(
    queries,
    new_kv,
    cache_pool,
    cache_len,
    local_pages,
    anchor,
    push_pages,
    prefill_attn,
    residual,
    out_weight,
    norm_gain,
    router,
    routes,
    gate_up,
    down_proj,
):
    columns = lax.axis_size("gy")
    slot_count = (MOVED + columns - 2) // (columns - 1)
    group_size = HEADS // KV_HEADS
    kv_width = 2 * KV_HEADS * HEAD
    query_heads = queries.reshape(R_DEV, KV_HEADS, group_size, HEAD)
    matches = (anchor[:, None] == jnp.arange(columns, dtype=jnp.int32)[None, :]).astype(jnp.int32)
    earlier = jnp.sum((jnp.cumsum(matches, axis=0) - 1) * matches, axis=1)
    chosen = anchor * slot_count + earlier
    local_max, local_totals, local_mix = paged_attend(
        queries[:LOCAL], local_pages, cache_len[:LOCAL], cache_pool
    )
    picker = chosen[:, None] == jnp.arange(columns * slot_count, dtype=jnp.int32)[None, :]
    sent_queries = jnp.einsum(
        "ms,md->sd",
        picker.astype(jnp.bfloat16),
        queries[LOCAL:],
        preferred_element_type=jnp.float32,
    )
    sent_lengths = jnp.sum(
        jnp.where(picker, cache_len[LOCAL:, None].astype(jnp.float32), 0.0), axis=0
    )
    got_queries, got_lengths = in_one_piece(
        (sent_queries.reshape(columns, slot_count, D), sent_lengths.reshape(columns, slot_count)),
        "gy",
        0,
        0,
        2,
    )
    far_max, far_totals, far_mix = paged_attend(
        got_queries.astype(jnp.bfloat16).reshape(columns * slot_count, D),
        push_pages,
        got_lengths.reshape(columns * slot_count).astype(jnp.int32),
        cache_pool,
    )
    back_max, back_totals, back_mix = in_one_piece(
        (
            far_max.reshape(columns, slot_count, KV_HEADS, group_size),
            far_totals.reshape(columns, slot_count, KV_HEADS, group_size),
            far_mix.reshape(columns, slot_count, KV_HEADS, group_size, HEAD),
        ),
        "gy",
        0,
        0,
        4,
    )
    cache_max = jnp.concatenate(
        [local_max, back_max.reshape(columns * slot_count, KV_HEADS, group_size)[chosen]], axis=0
    )
    totals = jnp.concatenate(
        [local_totals, back_totals.reshape(columns * slot_count, KV_HEADS, group_size)[chosen]],
        axis=0,
    )
    mixture = jnp.concatenate(
        [local_mix, back_mix.reshape(columns * slot_count, KV_HEADS, group_size, HEAD)[chosen]],
        axis=0,
    )
    attended = finish(query_heads, new_kv, cache_max, totals, mixture)
    tokens = jnp.concatenate([attended, prefill_attn], axis=0)
    row_count = tokens.shape[0]
    full_out = lax.all_gather(out_weight, "gx", axis=0, tiled=True)
    full_pair = lax.all_gather(gate_up, "gx", axis=0, tiled=True)
    full_down = lax.all_gather(down_proj, "gx", axis=0, tiled=True)
    stream = residual.astype(jnp.float32) + jnp.dot(
        tokens, full_out, preferred_element_type=jnp.float32
    )
    normed = (
        stream
        * lax.rsqrt(jnp.mean(stream * stream, axis=1, keepdims=True) + 1e-06)
        * norm_gain.astype(jnp.float32)
    ).astype(jnp.bfloat16)
    logits = jnp.dot(normed, router, preferred_element_type=jnp.float32)
    selector = routes[:, :, None] == jnp.arange(EXPERTS, dtype=jnp.int32)[None, None, :]
    gate_weights = jax.nn.softmax(
        jnp.sum(jnp.where(selector, logits[:, None, :], 0.0), axis=2), axis=1
    )
    row_hits = jnp.any(selector, axis=1)
    earlier_rows = (
        lax.broadcasted_iota(jnp.int32, (row_count, row_count), 1)
        < lax.broadcasted_iota(jnp.int32, (row_count, row_count), 0)
    ).astype(jnp.bfloat16)
    counts = jnp.dot(
        earlier_rows, row_hits.astype(jnp.bfloat16), preferred_element_type=jnp.float32
    ).astype(jnp.int32)
    place_of = jnp.sum(jnp.where(selector, counts[:, None, :], 0), axis=2)
    experts_dev = full_pair.shape[1]
    slot_hits = row_hits.T[:, None, :] & (
        counts.T[:, None, :] == jnp.arange(CAP, dtype=jnp.int32)[None, :, None]
    )
    chunk_hits = slot_hits.reshape(columns, experts_dev, CAP, row_count)
    returned_parts = []
    for local in range(experts_dev):
        outgoing = jnp.einsum(
            "scr,rd->scd",
            chunk_hits[:, local].astype(jnp.bfloat16),
            normed,
            preferred_element_type=jnp.float32,
        ).astype(jnp.bfloat16)
        arrived = lax.all_to_all(outgoing, "gy", split_axis=0, concat_axis=0, tiled=True)
        gate_pair = jnp.einsum(
            "scd,df->scf", arrived, full_pair[:, local], preferred_element_type=jnp.float32
        )
        hidden = (jax.nn.silu(gate_pair[..., :FF]) * gate_pair[..., FF:]).astype(jnp.bfloat16)
        expert_rows = jnp.einsum(
            "scf,df->scd", hidden, full_down[:, local], preferred_element_type=jnp.float32
        ).astype(jnp.bfloat16)
        returned_parts.append(
            lax.all_to_all(expert_rows, "gy", split_axis=0, concat_axis=0, tiled=True)
        )
    mixed = None
    for local, part in enumerate(returned_parts):
        spot = jnp.where(routes % experts_dev == local, routes // experts_dev * CAP + place_of, -1)
        gate_spot = jnp.sum(
            jnp.where(
                spot[:, :, None] == jnp.arange(columns * CAP, dtype=jnp.int32)[None, None, :],
                gate_weights[:, :, None],
                0.0,
            ),
            axis=1,
        )
        share = jnp.dot(
            gate_spot,
            part.reshape(columns * CAP, D),
            precision=lax.Precision.HIGHEST,
            preferred_element_type=jnp.float32,
        )
        mixed = share if mixed is None else mixed + share
    layer_out = stream + mixed
    return (attended, layer_out)


def solution(mesh):
    placed = (
        P(("gx", "gy"), None),
        P(("gx", "gy"), None),
        P(("gx", "gy"), None, None),
        P(("gx", "gy")),
        P(("gx", "gy"), None),
        P(("gx", "gy")),
        P(("gx", "gy"), None),
        P(("gx", "gy"), None),
        P(("gx", "gy"), None),
        P("gx", None),
        P(),
        P(),
        P(("gx", "gy"), None),
        P("gx", "gy", None),
        P("gx", "gy", None),
    )
    return jax.shard_map(
        body,
        mesh=mesh,
        in_specs=placed,
        out_specs=(P(("gx", "gy"), None), P(("gx", "gy"), None)),
        check_vma=False,
    )
```

```python
import math

import jax
import jax.numpy as jnp
from jax import lax
from jax.sharding import PartitionSpec as P
from jax.experimental import pallas as pl
from jax.experimental.pallas import tpu as pltpu

D = 1536
HEADS = 24
KV_HEADS = 8
HEAD = 64
EXPERTS = 32
FF = 512
TOP = 8
MAXLEN = 512
R_DEV = 16
LOCAL = 8
MOVED = 8
CAP = 48
NPAGE = 32
PAGE = 16


def attend_kernel(tables, lengths, q_ref, pool_ref, max_ref, tot_ref, mix_ref, kvbuf, sems):
    r = pl.program_id(0)
    n = pl.num_programs(0)
    half = KV_HEADS * HEAD

    def pages_of(req):
        return (lengths[req] + PAGE - 1) // PAGE

    def page_copy(req, slot, p):
        return pltpu.make_async_copy(
            pool_ref.at[tables[req, p]], kvbuf.at[slot, p], sems.at[slot, p]
        )

    def start(req, slot):
        def one(p, carry):
            page_copy(req, slot, p).start()
            return carry

        lax.fori_loop(0, pages_of(req), one, 0)

    @pl.when(r == 0)
    def _():
        kvbuf[...] = jnp.zeros(kvbuf.shape, kvbuf.dtype)
        start(0, 0)

    slot = r % 2

    @pl.when(r + 1 < n)
    def _():
        start(r + 1, 1 - slot)

    def wait_one(p, carry):
        page_copy(r, slot, p).wait()
        return carry

    lax.fori_loop(0, pages_of(r), wait_one, 0)
    kv = kvbuf.at[slot]
    keys = kv[:, :, :half].reshape(MAXLEN, half)
    values = kv[:, :, half:].reshape(MAXLEN, half)
    q = q_ref[0]
    scores = lax.dot_general(
        q, keys, (((1,), (1,)), ((), ())), preferred_element_type=jnp.float32
    ) * (1.0 / math.sqrt(HEAD))
    valid = lax.broadcasted_iota(jnp.int32, scores.shape, 1) < lengths[r]
    masked = jnp.where(valid, scores, -1e30)
    top = jnp.max(masked, axis=1, keepdims=True)
    expos = jnp.where(valid, jnp.exp(masked - top), 0.0)
    total = jnp.sum(expos, axis=1, keepdims=True)
    mix = jnp.dot(expos.astype(jnp.bfloat16), values, preferred_element_type=jnp.float32)
    max_ref[0] = jnp.broadcast_to(top, max_ref.shape[1:])
    tot_ref[0] = jnp.broadcast_to(total, tot_ref.shape[1:])
    group = lax.broadcasted_iota(jnp.int32, (HEADS, HEAD), 0) // (HEADS // KV_HEADS)
    picked = jnp.zeros((HEADS, HEAD), jnp.float32)
    for h in range(KV_HEADS):
        picked = picked + jnp.where(group == h, mix[:, h * HEAD : (h + 1) * HEAD], 0.0)
    mix_ref[0] = picked


def paged_attend(query_rows, tables, lengths, pool):
    count = query_rows.shape[0]
    group_size = HEADS // KV_HEADS
    half = KV_HEADS * HEAD
    heads = query_rows.reshape(count, KV_HEADS, group_size, 1, HEAD)
    mask = (jnp.arange(KV_HEADS)[:, None] == jnp.arange(KV_HEADS)[None, :])
    spread = jnp.where(
        mask[None, :, None, :, None], heads, jnp.zeros((), query_rows.dtype)
    ).reshape(count, HEADS, half)
    kv_width = pool.shape[2]
    grid_spec = pltpu.PrefetchScalarGridSpec(
        num_scalar_prefetch=2,
        grid=(count,),
        in_specs=[
            pl.BlockSpec((1, HEADS, half), lambda r, t, l: (r, 0, 0)),
            pl.BlockSpec(memory_space=pl.ANY),
        ],
        out_specs=[
            pl.BlockSpec((1, HEADS, 128), lambda r, t, l: (r, 0, 0)),
            pl.BlockSpec((1, HEADS, 128), lambda r, t, l: (r, 0, 0)),
            pl.BlockSpec((1, HEADS, HEAD), lambda r, t, l: (r, 0, 0)),
        ],
        scratch_shapes=[
            pltpu.VMEM((2, NPAGE, PAGE, kv_width), pool.dtype),
            pltpu.SemaphoreType.DMA((2, NPAGE)),
        ],
    )
    top, total, mix = pl.pallas_call(
        attend_kernel,
        grid_spec=grid_spec,
        out_shape=[
            jax.ShapeDtypeStruct((count, HEADS, 128), jnp.float32),
            jax.ShapeDtypeStruct((count, HEADS, 128), jnp.float32),
            jax.ShapeDtypeStruct((count, HEADS, HEAD), jnp.float32),
        ],
        compiler_params=pltpu.CompilerParams(dimension_semantics=("arbitrary",)),
        cost_estimate=pl.CostEstimate(
            flops=count * 4 * HEADS * MAXLEN * half,
            transcendentals=count * HEADS * MAXLEN,
            bytes_accessed=count * MAXLEN * kv_width * 2,
        ),
    )(tables, lengths, spread, pool)
    mixture = mix.reshape(count, KV_HEADS, group_size, HEAD)
    return (
        top[:, :, 0].reshape(count, KV_HEADS, group_size),
        total[:, :, 0].reshape(count, KV_HEADS, group_size),
        mixture,
    )


def in_one_piece(arrays, axis, split_dim, concat_dim, along):
    columns = [a.reshape(*a.shape[:along], -1) for a in arrays]
    both = jnp.concatenate(columns, axis=along)
    result, at, gathered = (
        lax.all_to_all(both, axis, split_axis=split_dim, concat_axis=concat_dim, tiled=True),
        0,
        [],
    )
    for a, column in zip(arrays, columns):
        share = result[..., at : at + column.shape[along]]
        gathered.append(share.reshape(*share.shape[:along], *a.shape[along:]))
        at += column.shape[along]
    return tuple(gathered)


def side_by_side(arrays, axis, dim, along):
    widths = [math.prod(a.shape[along:]) for a in arrays]
    both = jnp.concatenate(
        [a.reshape(*a.shape[:along], w) for a, w in zip(arrays, widths)], axis=along
    )
    result = lax.all_gather(both, axis, axis=dim, tiled=True)
    blocks = jnp.split(result, [sum(widths[:k]) for k in range(1, len(widths))], axis=along)
    return tuple(
        (b.reshape(*result.shape[:along], *a.shape[along:]) for a, b in zip(arrays, blocks))
    )


def partial_attend(query_heads, keyval, lengths):
    count_req, positions, kv_width = keyval.shape
    kv_count = query_heads.shape[1]
    head_size = query_heads.shape[3]
    half_width = kv_count * head_size
    key_rows = keyval[:, :, :half_width].reshape(count_req, positions, kv_count, head_size)
    value_rows = keyval[:, :, half_width:].reshape(count_req, positions, kv_count, head_size)
    scores = jnp.einsum(
        "nkgh,ntkh->nkgt", query_heads, key_rows, preferred_element_type=jnp.float32
    ) * (1.0 / math.sqrt(head_size))
    valid = (jnp.arange(positions)[None, :] < lengths[:, None])[:, None, None, :]
    masked = jnp.where(valid, scores, -1e30)
    cache_max = jnp.max(masked, axis=3)
    expos = jnp.where(valid, jnp.exp(masked - cache_max[..., None]), 0.0)
    totals = jnp.sum(expos, axis=3)
    weights = expos.astype(jnp.bfloat16)
    mixture = jnp.einsum("nkgt,ntkh->nkgh", weights, value_rows, preferred_element_type=jnp.float32)
    return (cache_max, totals, mixture)


def finish(query_heads, fresh, cache_max, totals, mixture):
    count_req, kv_count, group_size, head_size = query_heads.shape
    half_width = kv_count * head_size
    own_key = fresh[:, :half_width].reshape(count_req, kv_count, head_size)
    own_value = fresh[:, half_width:].reshape(count_req, kv_count, head_size).astype(jnp.float32)
    own_score = jnp.einsum(
        "nkgh,nkh->nkg", query_heads, own_key, preferred_element_type=jnp.float32
    ) * (1.0 / math.sqrt(head_size))
    highest = jnp.maximum(cache_max, own_score)
    old_share = jnp.exp(cache_max - highest)
    new_share = jnp.exp(own_score - highest)
    weighted = old_share[..., None] * mixture + new_share[..., None] * own_value[:, :, None, :]
    output = weighted / (old_share * totals + new_share)[..., None]
    return output.reshape(count_req, kv_count * group_size * head_size).astype(jnp.bfloat16)


def body(
    queries,
    new_kv,
    cache_pool,
    cache_len,
    local_pages,
    anchor,
    push_pages,
    prefill_attn,
    residual,
    out_weight,
    norm_gain,
    router,
    routes,
    gate_up,
    down_proj,
):
    columns = lax.axis_size("gy")
    slot_count = (MOVED + columns - 2) // (columns - 1)
    group_size = HEADS // KV_HEADS
    kv_width = 2 * KV_HEADS * HEAD
    query_heads = queries.reshape(R_DEV, KV_HEADS, group_size, HEAD)
    matches = (anchor[:, None] == jnp.arange(columns, dtype=jnp.int32)[None, :]).astype(jnp.int32)
    earlier = jnp.sum((jnp.cumsum(matches, axis=0) - 1) * matches, axis=1)
    chosen = anchor * slot_count + earlier
    local_max, local_totals, local_mix = paged_attend(
        queries[:LOCAL], local_pages, cache_len[:LOCAL], cache_pool
    )
    picker = chosen[:, None] == jnp.arange(columns * slot_count, dtype=jnp.int32)[None, :]
    sent_queries = jnp.einsum(
        "ms,md->sd",
        picker.astype(jnp.bfloat16),
        queries[LOCAL:],
        preferred_element_type=jnp.float32,
    )
    sent_lengths = jnp.sum(
        jnp.where(picker, cache_len[LOCAL:, None].astype(jnp.float32), 0.0), axis=0
    )
    got_queries, got_lengths = in_one_piece(
        (sent_queries.reshape(columns, slot_count, D), sent_lengths.reshape(columns, slot_count)),
        "gy",
        0,
        0,
        2,
    )
    far_max, far_totals, far_mix = paged_attend(
        got_queries.astype(jnp.bfloat16).reshape(columns * slot_count, D),
        push_pages,
        got_lengths.reshape(columns * slot_count).astype(jnp.int32),
        cache_pool,
    )
    back_max, back_totals, back_mix = in_one_piece(
        (
            far_max.reshape(columns, slot_count, KV_HEADS, group_size),
            far_totals.reshape(columns, slot_count, KV_HEADS, group_size),
            far_mix.reshape(columns, slot_count, KV_HEADS, group_size, HEAD),
        ),
        "gy",
        0,
        0,
        4,
    )
    cache_max = jnp.concatenate(
        [local_max, back_max.reshape(columns * slot_count, KV_HEADS, group_size)[chosen]], axis=0
    )
    totals = jnp.concatenate(
        [local_totals, back_totals.reshape(columns * slot_count, KV_HEADS, group_size)[chosen]],
        axis=0,
    )
    mixture = jnp.concatenate(
        [local_mix, back_mix.reshape(columns * slot_count, KV_HEADS, group_size, HEAD)[chosen]],
        axis=0,
    )
    attended = finish(query_heads, new_kv, cache_max, totals, mixture)
    tokens = jnp.concatenate([attended, prefill_attn], axis=0)
    row_count = tokens.shape[0]
    full_out = lax.all_gather(out_weight, "gx", axis=0, tiled=True)
    full_pair = lax.all_gather(gate_up, "gx", axis=0, tiled=True)
    full_down = lax.all_gather(down_proj, "gx", axis=0, tiled=True)
    stream = residual.astype(jnp.float32) + jnp.dot(
        tokens, full_out, preferred_element_type=jnp.float32
    )
    normed = (
        stream
        * lax.rsqrt(jnp.mean(stream * stream, axis=1, keepdims=True) + 1e-06)
        * norm_gain.astype(jnp.float32)
    ).astype(jnp.bfloat16)
    logits = jnp.dot(normed, router, preferred_element_type=jnp.float32)
    selector = routes[:, :, None] == jnp.arange(EXPERTS, dtype=jnp.int32)[None, None, :]
    gate_weights = jax.nn.softmax(
        jnp.sum(jnp.where(selector, logits[:, None, :], 0.0), axis=2), axis=1
    )
    row_hits = jnp.any(selector, axis=1)
    earlier_rows = (
        lax.broadcasted_iota(jnp.int32, (row_count, row_count), 1)
        < lax.broadcasted_iota(jnp.int32, (row_count, row_count), 0)
    ).astype(jnp.bfloat16)
    counts = jnp.dot(
        earlier_rows, row_hits.astype(jnp.bfloat16), preferred_element_type=jnp.float32
    ).astype(jnp.int32)
    place_of = jnp.sum(jnp.where(selector, counts[:, None, :], 0), axis=2)
    experts_dev = full_pair.shape[1]
    slot_hits = row_hits.T[:, None, :] & (
        counts.T[:, None, :] == jnp.arange(CAP, dtype=jnp.int32)[None, :, None]
    )
    chunk_hits = slot_hits.reshape(columns, experts_dev, CAP, row_count)
    returned_parts = []
    for local in range(experts_dev):
        outgoing = jnp.einsum(
            "scr,rd->scd",
            chunk_hits[:, local].astype(jnp.bfloat16),
            normed,
            preferred_element_type=jnp.float32,
        ).astype(jnp.bfloat16)
        arrived = lax.all_to_all(outgoing, "gy", split_axis=0, concat_axis=0, tiled=True)
        gate_pair = jnp.einsum(
            "scd,df->scf", arrived, full_pair[:, local], preferred_element_type=jnp.float32
        )
        hidden = (jax.nn.silu(gate_pair[..., :FF]) * gate_pair[..., FF:]).astype(jnp.bfloat16)
        expert_rows = jnp.einsum(
            "scf,df->scd", hidden, full_down[:, local], preferred_element_type=jnp.float32
        ).astype(jnp.bfloat16)
        returned_parts.append(
            lax.all_to_all(expert_rows, "gy", split_axis=0, concat_axis=0, tiled=True)
        )
    flat_place = place_of.reshape(row_count * TOP)
    flat_expert = routes.reshape(row_count * TOP)
    picked = None
    for local, part in enumerate(returned_parts):
        spot = jnp.where(
            flat_expert % experts_dev == local, flat_expert // experts_dev * CAP + flat_place, -1
        )
        one_hot = (spot[:, None] == jnp.arange(columns * CAP, dtype=jnp.int32)[None, :]).astype(
            jnp.bfloat16
        )
        share = jnp.dot(
            one_hot, part.reshape(columns * CAP, D), preferred_element_type=jnp.float32
        )
        picked = share if picked is None else picked + share
    picked = picked.reshape(row_count, TOP, D)
    layer_out = stream + jnp.sum(gate_weights[:, :, None] * picked, axis=1)
    return (attended, layer_out)


def solution(mesh):
    placed = (
        P(("gx", "gy"), None),
        P(("gx", "gy"), None),
        P(("gx", "gy"), None, None),
        P(("gx", "gy")),
        P(("gx", "gy"), None),
        P(("gx", "gy")),
        P(("gx", "gy"), None),
        P(("gx", "gy"), None),
        P(("gx", "gy"), None),
        P("gx", None),
        P(),
        P(),
        P(("gx", "gy"), None),
        P("gx", "gy", None),
        P("gx", "gy", None),
    )
    return jax.shard_map(
        body,
        mesh=mesh,
        in_specs=placed,
        out_specs=(P(("gx", "gy"), None), P(("gx", "gy"), None)),
        check_vma=False,
    )
```

```python
import math

import jax
import jax.numpy as jnp
from jax import lax
from jax.sharding import PartitionSpec as P
from jax.experimental import pallas as pl
from jax.experimental.pallas import tpu as pltpu

D = 1536
HEADS = 24
KV_HEADS = 8
HEAD = 64
EXPERTS = 32
FF = 512
TOP = 8
MAXLEN = 512
R_DEV = 16
LOCAL = 8
MOVED = 8
CAP = 48
NPAGE = 32
PAGE = 16


def attend_kernel(tables, lengths, q_ref, pool_ref, max_ref, tot_ref, mix_ref, kvbuf, sems):
    r = pl.program_id(0)
    n = pl.num_programs(0)
    half = KV_HEADS * HEAD

    def pages_of(req):
        return (lengths[req] + PAGE - 1) // PAGE

    def page_copy(req, slot, p):
        return pltpu.make_async_copy(
            pool_ref.at[tables[req, p]], kvbuf.at[slot, p], sems.at[slot, p]
        )

    def start(req, slot):
        def one(p, carry):
            page_copy(req, slot, p).start()
            return carry

        lax.fori_loop(0, pages_of(req), one, 0)

    @pl.when(r == 0)
    def _():
        kvbuf[...] = jnp.zeros(kvbuf.shape, kvbuf.dtype)
        start(0, 0)

    slot = r % 2

    @pl.when(r + 1 < n)
    def _():
        start(r + 1, 1 - slot)

    def wait_one(p, carry):
        page_copy(r, slot, p).wait()
        return carry

    lax.fori_loop(0, pages_of(r), wait_one, 0)
    @pl.when(lengths[r] == 0)
    def _():
        max_ref[...] = jnp.full(max_ref.shape, -1e30, max_ref.dtype)
        tot_ref[...] = jnp.zeros(tot_ref.shape, tot_ref.dtype)
        mix_ref[...] = jnp.zeros(mix_ref.shape, mix_ref.dtype)

    @pl.when(lengths[r] > 0)
    def _():
        kv = kvbuf.at[slot]
        keys = kv[:, :, :half].reshape(MAXLEN, half)
        values = kv[:, :, half:].reshape(MAXLEN, half)
        q = q_ref[0]
        scores = lax.dot_general(
            q, keys, (((1,), (1,)), ((), ())), preferred_element_type=jnp.float32
        ) * (1.0 / math.sqrt(HEAD))
        valid = lax.broadcasted_iota(jnp.int32, scores.shape, 1) < lengths[r]
        masked = jnp.where(valid, scores, -1e30)
        top = jnp.max(masked, axis=1, keepdims=True)
        expos = jnp.where(valid, jnp.exp(masked - top), 0.0)
        total = jnp.sum(expos, axis=1, keepdims=True)
        mix = jnp.dot(expos.astype(jnp.bfloat16), values, preferred_element_type=jnp.float32)
        max_ref[0] = jnp.broadcast_to(top, max_ref.shape[1:])
        tot_ref[0] = jnp.broadcast_to(total, tot_ref.shape[1:])
        mix_ref[0] = mix


def paged_attend(query_rows, tables, lengths, pool):
    count = query_rows.shape[0]
    group_size = HEADS // KV_HEADS
    half = KV_HEADS * HEAD
    heads = query_rows.reshape(count, KV_HEADS, group_size, 1, HEAD)
    mask = (jnp.arange(KV_HEADS)[:, None] == jnp.arange(KV_HEADS)[None, :])
    spread = jnp.where(
        mask[None, :, None, :, None], heads, jnp.zeros((), query_rows.dtype)
    ).reshape(count, HEADS, half)
    kv_width = pool.shape[2]
    grid_spec = pltpu.PrefetchScalarGridSpec(
        num_scalar_prefetch=2,
        grid=(count,),
        in_specs=[
            pl.BlockSpec((1, HEADS, half), lambda r, t, l: (r, 0, 0)),
            pl.BlockSpec(memory_space=pl.ANY),
        ],
        out_specs=[
            pl.BlockSpec((1, HEADS, 128), lambda r, t, l: (r, 0, 0)),
            pl.BlockSpec((1, HEADS, 128), lambda r, t, l: (r, 0, 0)),
            pl.BlockSpec((1, HEADS, half), lambda r, t, l: (r, 0, 0)),
        ],
        scratch_shapes=[
            pltpu.VMEM((2, NPAGE, PAGE, kv_width), pool.dtype),
            pltpu.SemaphoreType.DMA((2, NPAGE)),
        ],
    )
    top, total, mix = pl.pallas_call(
        attend_kernel,
        grid_spec=grid_spec,
        out_shape=[
            jax.ShapeDtypeStruct((count, HEADS, 128), jnp.float32),
            jax.ShapeDtypeStruct((count, HEADS, 128), jnp.float32),
            jax.ShapeDtypeStruct((count, HEADS, half), jnp.float32),
        ],
        compiler_params=pltpu.CompilerParams(dimension_semantics=("arbitrary",)),
        cost_estimate=pl.CostEstimate(
            flops=count * 4 * HEADS * MAXLEN * half,
            transcendentals=count * HEADS * MAXLEN,
            bytes_accessed=count * MAXLEN * kv_width * 2,
        ),
    )(tables, lengths, spread, pool)
    blocks = mix.reshape(count, KV_HEADS, group_size, KV_HEADS, HEAD)
    mixture = jnp.sum(jnp.where(mask[None, :, None, :, None], blocks, 0.0), axis=3)
    return (
        top[:, :, 0].reshape(count, KV_HEADS, group_size),
        total[:, :, 0].reshape(count, KV_HEADS, group_size),
        mixture,
    )


def in_one_piece(arrays, axis, split_dim, concat_dim, along):
    columns = [a.reshape(*a.shape[:along], -1) for a in arrays]
    both = jnp.concatenate(columns, axis=along)
    result, at, gathered = (
        lax.all_to_all(both, axis, split_axis=split_dim, concat_axis=concat_dim, tiled=True),
        0,
        [],
    )
    for a, column in zip(arrays, columns):
        share = result[..., at : at + column.shape[along]]
        gathered.append(share.reshape(*share.shape[:along], *a.shape[along:]))
        at += column.shape[along]
    return tuple(gathered)


def side_by_side(arrays, axis, dim, along):
    widths = [math.prod(a.shape[along:]) for a in arrays]
    both = jnp.concatenate(
        [a.reshape(*a.shape[:along], w) for a, w in zip(arrays, widths)], axis=along
    )
    result = lax.all_gather(both, axis, axis=dim, tiled=True)
    blocks = jnp.split(result, [sum(widths[:k]) for k in range(1, len(widths))], axis=along)
    return tuple(
        (b.reshape(*result.shape[:along], *a.shape[along:]) for a, b in zip(arrays, blocks))
    )


def partial_attend(query_heads, keyval, lengths):
    count_req, positions, kv_width = keyval.shape
    kv_count = query_heads.shape[1]
    head_size = query_heads.shape[3]
    half_width = kv_count * head_size
    key_rows = keyval[:, :, :half_width].reshape(count_req, positions, kv_count, head_size)
    value_rows = keyval[:, :, half_width:].reshape(count_req, positions, kv_count, head_size)
    scores = jnp.einsum(
        "nkgh,ntkh->nkgt", query_heads, key_rows, preferred_element_type=jnp.float32
    ) * (1.0 / math.sqrt(head_size))
    valid = (jnp.arange(positions)[None, :] < lengths[:, None])[:, None, None, :]
    masked = jnp.where(valid, scores, -1e30)
    cache_max = jnp.max(masked, axis=3)
    expos = jnp.where(valid, jnp.exp(masked - cache_max[..., None]), 0.0)
    totals = jnp.sum(expos, axis=3)
    weights = expos.astype(jnp.bfloat16)
    mixture = jnp.einsum("nkgt,ntkh->nkgh", weights, value_rows, preferred_element_type=jnp.float32)
    return (cache_max, totals, mixture)


def finish(query_heads, fresh, cache_max, totals, mixture):
    count_req, kv_count, group_size, head_size = query_heads.shape
    half_width = kv_count * head_size
    own_key = fresh[:, :half_width].reshape(count_req, kv_count, head_size)
    own_value = fresh[:, half_width:].reshape(count_req, kv_count, head_size).astype(jnp.float32)
    own_score = jnp.einsum(
        "nkgh,nkh->nkg", query_heads, own_key, preferred_element_type=jnp.float32
    ) * (1.0 / math.sqrt(head_size))
    highest = jnp.maximum(cache_max, own_score)
    old_share = jnp.exp(cache_max - highest)
    new_share = jnp.exp(own_score - highest)
    weighted = old_share[..., None] * mixture + new_share[..., None] * own_value[:, :, None, :]
    output = weighted / (old_share * totals + new_share)[..., None]
    return output.reshape(count_req, kv_count * group_size * head_size).astype(jnp.bfloat16)


def body(
    queries,
    new_kv,
    cache_pool,
    cache_len,
    local_pages,
    anchor,
    push_pages,
    prefill_attn,
    residual,
    out_weight,
    norm_gain,
    router,
    routes,
    gate_up,
    down_proj,
):
    columns = lax.axis_size("gy")
    slot_count = (MOVED + columns - 2) // (columns - 1)
    group_size = HEADS // KV_HEADS
    kv_width = 2 * KV_HEADS * HEAD
    query_heads = queries.reshape(R_DEV, KV_HEADS, group_size, HEAD)
    matches = (anchor[:, None] == jnp.arange(columns, dtype=jnp.int32)[None, :]).astype(jnp.int32)
    earlier = jnp.sum((jnp.cumsum(matches, axis=0) - 1) * matches, axis=1)
    chosen = anchor * slot_count + earlier
    local_max, local_totals, local_mix = paged_attend(
        queries[:LOCAL], local_pages, cache_len[:LOCAL], cache_pool
    )
    picker = chosen[:, None] == jnp.arange(columns * slot_count, dtype=jnp.int32)[None, :]
    sent_queries = jnp.einsum(
        "ms,md->sd",
        picker.astype(jnp.bfloat16),
        queries[LOCAL:],
        preferred_element_type=jnp.float32,
    )
    sent_lengths = jnp.sum(
        jnp.where(picker, cache_len[LOCAL:, None].astype(jnp.float32), 0.0), axis=0
    )
    got_queries, got_lengths = in_one_piece(
        (sent_queries.reshape(columns, slot_count, D), sent_lengths.reshape(columns, slot_count)),
        "gy",
        0,
        0,
        2,
    )
    far_max, far_totals, far_mix = paged_attend(
        got_queries.astype(jnp.bfloat16).reshape(columns * slot_count, D),
        push_pages,
        got_lengths.reshape(columns * slot_count).astype(jnp.int32),
        cache_pool,
    )
    back_max, back_totals, back_mix = in_one_piece(
        (
            far_max.reshape(columns, slot_count, KV_HEADS, group_size),
            far_totals.reshape(columns, slot_count, KV_HEADS, group_size),
            far_mix.reshape(columns, slot_count, KV_HEADS, group_size, HEAD),
        ),
        "gy",
        0,
        0,
        4,
    )
    cache_max = jnp.concatenate(
        [local_max, back_max.reshape(columns * slot_count, KV_HEADS, group_size)[chosen]], axis=0
    )
    totals = jnp.concatenate(
        [local_totals, back_totals.reshape(columns * slot_count, KV_HEADS, group_size)[chosen]],
        axis=0,
    )
    mixture = jnp.concatenate(
        [local_mix, back_mix.reshape(columns * slot_count, KV_HEADS, group_size, HEAD)[chosen]],
        axis=0,
    )
    attended = finish(query_heads, new_kv, cache_max, totals, mixture)
    tokens = jnp.concatenate([attended, prefill_attn], axis=0)
    row_count = tokens.shape[0]
    full_out = lax.all_gather(out_weight, "gx", axis=0, tiled=True)
    full_pair = lax.all_gather(gate_up, "gx", axis=0, tiled=True)
    full_down = lax.all_gather(down_proj, "gx", axis=0, tiled=True)
    stream = residual.astype(jnp.float32) + jnp.dot(
        tokens, full_out, preferred_element_type=jnp.float32
    )
    normed = (
        stream
        * lax.rsqrt(jnp.mean(stream * stream, axis=1, keepdims=True) + 1e-06)
        * norm_gain.astype(jnp.float32)
    ).astype(jnp.bfloat16)
    logits = jnp.dot(normed, router, preferred_element_type=jnp.float32)
    selector = routes[:, :, None] == jnp.arange(EXPERTS, dtype=jnp.int32)[None, None, :]
    gate_weights = jax.nn.softmax(
        jnp.sum(jnp.where(selector, logits[:, None, :], 0.0), axis=2), axis=1
    )
    row_hits = jnp.any(selector, axis=1)
    earlier_rows = (
        lax.broadcasted_iota(jnp.int32, (row_count, row_count), 1)
        < lax.broadcasted_iota(jnp.int32, (row_count, row_count), 0)
    ).astype(jnp.bfloat16)
    counts = jnp.dot(
        earlier_rows, row_hits.astype(jnp.bfloat16), preferred_element_type=jnp.float32
    ).astype(jnp.int32)
    place_of = jnp.sum(jnp.where(selector, counts[:, None, :], 0), axis=2)
    experts_dev = full_pair.shape[1]
    slot_hits = row_hits.T[:, None, :] & (
        counts.T[:, None, :] == jnp.arange(CAP, dtype=jnp.int32)[None, :, None]
    )
    chunk_hits = slot_hits.reshape(columns, experts_dev, CAP, row_count)
    returned_parts = []
    for local in range(experts_dev):
        outgoing = jnp.einsum(
            "scr,rd->scd",
            chunk_hits[:, local].astype(jnp.bfloat16),
            normed,
            preferred_element_type=jnp.float32,
        ).astype(jnp.bfloat16)
        arrived = lax.all_to_all(outgoing, "gy", split_axis=0, concat_axis=0, tiled=True)
        gate_pair = jnp.einsum(
            "scd,df->scf", arrived, full_pair[:, local], preferred_element_type=jnp.float32
        )
        hidden = (jax.nn.silu(gate_pair[..., :FF]) * gate_pair[..., FF:]).astype(jnp.bfloat16)
        expert_rows = jnp.einsum(
            "scf,df->scd", hidden, full_down[:, local], preferred_element_type=jnp.float32
        ).astype(jnp.bfloat16)
        returned_parts.append(
            lax.all_to_all(expert_rows, "gy", split_axis=0, concat_axis=0, tiled=True)
        )
    flat_place = place_of.reshape(row_count * TOP)
    flat_expert = routes.reshape(row_count * TOP)
    picked = None
    for local, part in enumerate(returned_parts):
        spot = jnp.where(
            flat_expert % experts_dev == local, flat_expert // experts_dev * CAP + flat_place, -1
        )
        one_hot = (spot[:, None] == jnp.arange(columns * CAP, dtype=jnp.int32)[None, :]).astype(
            jnp.bfloat16
        )
        share = jnp.dot(
            one_hot, part.reshape(columns * CAP, D), preferred_element_type=jnp.float32
        )
        picked = share if picked is None else picked + share
    picked = picked.reshape(row_count, TOP, D)
    layer_out = stream + jnp.sum(gate_weights[:, :, None] * picked, axis=1)
    return (attended, layer_out)


def solution(mesh):
    placed = (
        P(("gx", "gy"), None),
        P(("gx", "gy"), None),
        P(("gx", "gy"), None, None),
        P(("gx", "gy")),
        P(("gx", "gy"), None),
        P(("gx", "gy")),
        P(("gx", "gy"), None),
        P(("gx", "gy"), None),
        P(("gx", "gy"), None),
        P("gx", None),
        P(),
        P(),
        P(("gx", "gy"), None),
        P("gx", "gy", None),
        P("gx", "gy", None),
    )
    return jax.shard_map(
        body,
        mesh=mesh,
        in_specs=placed,
        out_specs=(P(("gx", "gy"), None), P(("gx", "gy"), None)),
        check_vma=False,
    )
```

```python
import math

import jax
import jax.numpy as jnp
from jax import lax
from jax.sharding import PartitionSpec as P
from jax.experimental import pallas as pl
from jax.experimental.pallas import tpu as pltpu

D = 1536
HEADS = 24
KV_HEADS = 8
HEAD = 64
EXPERTS = 32
FF = 512
TOP = 8
MAXLEN = 512
R_DEV = 16
LOCAL = 8
MOVED = 8
CAP = 48
NPAGE = 32
PAGE = 16


def attend_kernel(tables, lengths, q_ref, pool_ref, max_ref, tot_ref, mix_ref, kvbuf, sems):
    r = pl.program_id(0)
    n = pl.num_programs(0)
    half = KV_HEADS * HEAD

    def pages_of(req):
        return (lengths[req] + PAGE - 1) // PAGE

    def page_copy(req, slot, p):
        return pltpu.make_async_copy(
            pool_ref.at[tables[req, p]], kvbuf.at[slot, p], sems.at[slot, p]
        )

    def start(req, slot):
        def one(p, carry):
            page_copy(req, slot, p).start()
            return carry

        lax.fori_loop(0, pages_of(req), one, 0)

    @pl.when(r == 0)
    def _():
        kvbuf[...] = jnp.zeros(kvbuf.shape, kvbuf.dtype)
        start(0, 0)

    slot = r % 2

    @pl.when(r + 1 < n)
    def _():
        start(r + 1, 1 - slot)

    def wait_one(p, carry):
        page_copy(r, slot, p).wait()
        return carry

    lax.fori_loop(0, pages_of(r), wait_one, 0)
    @pl.when(lengths[r] == 0)
    def _():
        max_ref[...] = jnp.full(max_ref.shape, -1e30, max_ref.dtype)
        tot_ref[...] = jnp.zeros(tot_ref.shape, tot_ref.dtype)
        mix_ref[...] = jnp.zeros(mix_ref.shape, mix_ref.dtype)

    @pl.when(lengths[r] > 0)
    def _():
        kv = kvbuf.at[slot]
        keys = kv[:, :, :half].reshape(MAXLEN, half)
        values = kv[:, :, half:].reshape(MAXLEN, half)
        q = q_ref[0]
        scores = lax.dot_general(
            q, keys, (((1,), (1,)), ((), ())), preferred_element_type=jnp.float32
        ) * (1.0 / math.sqrt(HEAD))
        valid = lax.broadcasted_iota(jnp.int32, scores.shape, 1) < lengths[r]
        masked = jnp.where(valid, scores, -1e30)
        top = jnp.max(masked, axis=1, keepdims=True)
        expos = jnp.where(valid, jnp.exp(masked - top), 0.0)
        total = jnp.sum(expos, axis=1, keepdims=True)
        mix = jnp.dot(expos.astype(jnp.bfloat16), values, preferred_element_type=jnp.float32)
        max_ref[0] = jnp.broadcast_to(top, max_ref.shape[1:])
        tot_ref[0] = jnp.broadcast_to(total, tot_ref.shape[1:])
        mix_ref[0] = mix


def paged_attend(query_rows, tables, lengths, pool):
    count = query_rows.shape[0]
    group_size = HEADS // KV_HEADS
    half = KV_HEADS * HEAD
    heads = query_rows.reshape(count, KV_HEADS, group_size, 1, HEAD)
    mask = (jnp.arange(KV_HEADS)[:, None] == jnp.arange(KV_HEADS)[None, :])
    spread = jnp.where(
        mask[None, :, None, :, None], heads, jnp.zeros((), query_rows.dtype)
    ).reshape(count, HEADS, half)
    kv_width = pool.shape[2]
    grid_spec = pltpu.PrefetchScalarGridSpec(
        num_scalar_prefetch=2,
        grid=(count,),
        in_specs=[
            pl.BlockSpec((1, HEADS, half), lambda r, t, l: (r, 0, 0)),
            pl.BlockSpec(memory_space=pl.ANY),
        ],
        out_specs=[
            pl.BlockSpec((1, HEADS, 128), lambda r, t, l: (r, 0, 0)),
            pl.BlockSpec((1, HEADS, 128), lambda r, t, l: (r, 0, 0)),
            pl.BlockSpec((1, HEADS, half), lambda r, t, l: (r, 0, 0)),
        ],
        scratch_shapes=[
            pltpu.VMEM((2, NPAGE, PAGE, kv_width), pool.dtype),
            pltpu.SemaphoreType.DMA((2, NPAGE)),
        ],
    )
    top, total, mix = pl.pallas_call(
        attend_kernel,
        grid_spec=grid_spec,
        out_shape=[
            jax.ShapeDtypeStruct((count, HEADS, 128), jnp.float32),
            jax.ShapeDtypeStruct((count, HEADS, 128), jnp.float32),
            jax.ShapeDtypeStruct((count, HEADS, half), jnp.float32),
        ],
        compiler_params=pltpu.CompilerParams(dimension_semantics=("arbitrary",)),
        cost_estimate=pl.CostEstimate(
            flops=count * 4 * HEADS * MAXLEN * half,
            transcendentals=count * HEADS * MAXLEN,
            bytes_accessed=count * MAXLEN * kv_width * 2,
        ),
    )(tables, lengths, spread, pool)
    blocks = mix.reshape(count, KV_HEADS, group_size, KV_HEADS, HEAD)
    mixture = jnp.sum(jnp.where(mask[None, :, None, :, None], blocks, 0.0), axis=3)
    return (
        top[:, :, 0].reshape(count, KV_HEADS, group_size),
        total[:, :, 0].reshape(count, KV_HEADS, group_size),
        mixture,
    )


def in_one_piece(arrays, axis, split_dim, concat_dim, along):
    columns = [a.reshape(*a.shape[:along], -1) for a in arrays]
    both = jnp.concatenate(columns, axis=along)
    result, at, gathered = (
        lax.all_to_all(both, axis, split_axis=split_dim, concat_axis=concat_dim, tiled=True),
        0,
        [],
    )
    for a, column in zip(arrays, columns):
        share = result[..., at : at + column.shape[along]]
        gathered.append(share.reshape(*share.shape[:along], *a.shape[along:]))
        at += column.shape[along]
    return tuple(gathered)


def side_by_side(arrays, axis, dim, along):
    widths = [math.prod(a.shape[along:]) for a in arrays]
    both = jnp.concatenate(
        [a.reshape(*a.shape[:along], w) for a, w in zip(arrays, widths)], axis=along
    )
    result = lax.all_gather(both, axis, axis=dim, tiled=True)
    blocks = jnp.split(result, [sum(widths[:k]) for k in range(1, len(widths))], axis=along)
    return tuple(
        (b.reshape(*result.shape[:along], *a.shape[along:]) for a, b in zip(arrays, blocks))
    )


def partial_attend(query_heads, keyval, lengths):
    count_req, positions, kv_width = keyval.shape
    kv_count = query_heads.shape[1]
    head_size = query_heads.shape[3]
    half_width = kv_count * head_size
    key_rows = keyval[:, :, :half_width].reshape(count_req, positions, kv_count, head_size)
    value_rows = keyval[:, :, half_width:].reshape(count_req, positions, kv_count, head_size)
    scores = jnp.einsum(
        "nkgh,ntkh->nkgt", query_heads, key_rows, preferred_element_type=jnp.float32
    ) * (1.0 / math.sqrt(head_size))
    valid = (jnp.arange(positions)[None, :] < lengths[:, None])[:, None, None, :]
    masked = jnp.where(valid, scores, -1e30)
    cache_max = jnp.max(masked, axis=3)
    expos = jnp.where(valid, jnp.exp(masked - cache_max[..., None]), 0.0)
    totals = jnp.sum(expos, axis=3)
    weights = expos.astype(jnp.bfloat16)
    mixture = jnp.einsum("nkgt,ntkh->nkgh", weights, value_rows, preferred_element_type=jnp.float32)
    return (cache_max, totals, mixture)


def finish(query_heads, fresh, cache_max, totals, mixture):
    count_req, kv_count, group_size, head_size = query_heads.shape
    half_width = kv_count * head_size
    own_key = fresh[:, :half_width].reshape(count_req, kv_count, head_size)
    own_value = fresh[:, half_width:].reshape(count_req, kv_count, head_size).astype(jnp.float32)
    own_score = jnp.einsum(
        "nkgh,nkh->nkg", query_heads, own_key, preferred_element_type=jnp.float32
    ) * (1.0 / math.sqrt(head_size))
    highest = jnp.maximum(cache_max, own_score)
    old_share = jnp.exp(cache_max - highest)
    new_share = jnp.exp(own_score - highest)
    weighted = old_share[..., None] * mixture + new_share[..., None] * own_value[:, :, None, :]
    output = weighted / (old_share * totals + new_share)[..., None]
    return output.reshape(count_req, kv_count * group_size * head_size).astype(jnp.bfloat16)


def body(
    queries,
    new_kv,
    cache_pool,
    cache_len,
    local_pages,
    anchor,
    push_pages,
    prefill_attn,
    residual,
    out_weight,
    norm_gain,
    router,
    routes,
    gate_up,
    down_proj,
):
    columns = lax.axis_size("gy")
    slot_count = (MOVED + columns - 2) // (columns - 1)
    group_size = HEADS // KV_HEADS
    kv_width = 2 * KV_HEADS * HEAD
    query_heads = queries.reshape(R_DEV, KV_HEADS, group_size, HEAD)
    matches = (anchor[:, None] == jnp.arange(columns, dtype=jnp.int32)[None, :]).astype(jnp.int32)
    earlier = jnp.sum((jnp.cumsum(matches, axis=0) - 1) * matches, axis=1)
    chosen = anchor * slot_count + earlier
    local_max, local_totals, local_mix = paged_attend(
        queries[:LOCAL], local_pages, cache_len[:LOCAL], cache_pool
    )
    picker = chosen[:, None] == jnp.arange(columns * slot_count, dtype=jnp.int32)[None, :]
    sent_queries = jnp.einsum(
        "ms,md->sd",
        picker.astype(jnp.bfloat16),
        queries[LOCAL:],
        preferred_element_type=jnp.float32,
    )
    sent_lengths = jnp.sum(
        jnp.where(picker, cache_len[LOCAL:, None].astype(jnp.float32), 0.0), axis=0
    )
    got_queries, got_lengths = in_one_piece(
        (sent_queries.reshape(columns, slot_count, D), sent_lengths.reshape(columns, slot_count)),
        "gy",
        0,
        0,
        2,
    )
    far_max, far_totals, far_mix = paged_attend(
        got_queries.astype(jnp.bfloat16).reshape(columns * slot_count, D),
        push_pages,
        got_lengths.reshape(columns * slot_count).astype(jnp.int32),
        cache_pool,
    )
    back_max, back_totals, back_mix = in_one_piece(
        (
            far_max.reshape(columns, slot_count, KV_HEADS, group_size),
            far_totals.reshape(columns, slot_count, KV_HEADS, group_size),
            far_mix.reshape(columns, slot_count, KV_HEADS, group_size, HEAD),
        ),
        "gy",
        0,
        0,
        4,
    )
    cache_max = jnp.concatenate(
        [local_max, back_max.reshape(columns * slot_count, KV_HEADS, group_size)[chosen]], axis=0
    )
    totals = jnp.concatenate(
        [local_totals, back_totals.reshape(columns * slot_count, KV_HEADS, group_size)[chosen]],
        axis=0,
    )
    mixture = jnp.concatenate(
        [local_mix, back_mix.reshape(columns * slot_count, KV_HEADS, group_size, HEAD)[chosen]],
        axis=0,
    )
    attended = finish(query_heads, new_kv, cache_max, totals, mixture)
    tokens = jnp.concatenate([attended, prefill_attn], axis=0)
    row_count = tokens.shape[0]
    full_out = lax.all_gather(out_weight, "gx", axis=0, tiled=True)
    full_pair = lax.all_gather(gate_up, "gx", axis=0, tiled=True)
    full_down = lax.all_gather(down_proj, "gx", axis=0, tiled=True)
    stream = residual.astype(jnp.float32) + jnp.dot(
        tokens, full_out, preferred_element_type=jnp.float32
    )
    normed = (
        stream
        * lax.rsqrt(jnp.mean(stream * stream, axis=1, keepdims=True) + 1e-06)
        * norm_gain.astype(jnp.float32)
    ).astype(jnp.bfloat16)
    logits = jnp.dot(normed, router, preferred_element_type=jnp.float32)
    selector = routes[:, :, None] == jnp.arange(EXPERTS, dtype=jnp.int32)[None, None, :]
    gate_weights = jax.nn.softmax(
        jnp.sum(jnp.where(selector, logits[:, None, :], 0.0), axis=2), axis=1
    )
    row_hits = jnp.any(selector, axis=1)
    earlier_rows = (
        lax.broadcasted_iota(jnp.int32, (row_count, row_count), 1)
        < lax.broadcasted_iota(jnp.int32, (row_count, row_count), 0)
    ).astype(jnp.bfloat16)
    counts = jnp.dot(
        earlier_rows, row_hits.astype(jnp.bfloat16), preferred_element_type=jnp.float32
    ).astype(jnp.int32)
    place_of = jnp.sum(jnp.where(selector, counts[:, None, :], 0), axis=2)
    experts_dev = full_pair.shape[1]
    slot_hits = row_hits.T[:, None, :] & (
        counts.T[:, None, :] == jnp.arange(CAP, dtype=jnp.int32)[None, :, None]
    )
    chunk_hits = slot_hits.reshape(columns, experts_dev, CAP, row_count)
    returned_parts = []
    for local in range(experts_dev):
        outgoing = jnp.einsum(
            "scr,rd->scd",
            chunk_hits[:, local].astype(jnp.bfloat16),
            normed,
            preferred_element_type=jnp.float32,
        ).astype(jnp.bfloat16)
        arrived = lax.all_to_all(outgoing, "gy", split_axis=0, concat_axis=0, tiled=True)
        gate_pair = jnp.einsum(
            "scd,df->scf", arrived, full_pair[:, local], preferred_element_type=jnp.float32
        )
        hidden = (jax.nn.silu(gate_pair[..., :FF]) * gate_pair[..., FF:]).astype(jnp.bfloat16)
        expert_rows = jnp.einsum(
            "scf,df->scd", hidden, full_down[:, local], preferred_element_type=jnp.float32
        ).astype(jnp.bfloat16)
        returned_parts.append(
            lax.all_to_all(expert_rows, "gy", split_axis=0, concat_axis=0, tiled=True)
        )
    mixed = None
    for local, part in enumerate(returned_parts):
        spot = jnp.where(routes % experts_dev == local, routes // experts_dev * CAP + place_of, -1)
        gate_spot = jnp.sum(
            jnp.where(
                spot[:, :, None] == jnp.arange(columns * CAP, dtype=jnp.int32)[None, None, :],
                gate_weights[:, :, None],
                0.0,
            ),
            axis=1,
        )
        share = jnp.dot(
            gate_spot,
            part.reshape(columns * CAP, D),
            precision=lax.Precision.HIGHEST,
            preferred_element_type=jnp.float32,
        )
        mixed = share if mixed is None else mixed + share
    layer_out = stream + mixed
    return (attended, layer_out)


def solution(mesh):
    placed = (
        P(("gx", "gy"), None),
        P(("gx", "gy"), None),
        P(("gx", "gy"), None, None),
        P(("gx", "gy")),
        P(("gx", "gy"), None),
        P(("gx", "gy")),
        P(("gx", "gy"), None),
        P(("gx", "gy"), None),
        P(("gx", "gy"), None),
        P("gx", None),
        P(),
        P(),
        P(("gx", "gy"), None),
        P("gx", "gy", None),
        P("gx", "gy", None),
    )
    return jax.shard_map(
        body,
        mesh=mesh,
        in_specs=placed,
        out_specs=(P(("gx", "gy"), None), P(("gx", "gy"), None)),
        check_vma=False,
    )
```
